256 devices in a mesh: rows: 128 (over y, x, z), tok: 2 (over core).
Axes of the slice: x: 4, y: 4, z: 8, core: 2. Of those that a mesh axis runs over, the one named last changes fastest.
Arguments:
- calib: bfloat16 [128, 26752], P('tok'), may hold values from -6 to 6
- w_panels: bfloat16 [16384, 256], P(('rows', 'tok')), may hold values from -0.0390625 to 0.0390625
- w_trail: bfloat16 [16384, 26496], P(('rows', 'tok')), may hold values from -0.0390625 to 0.0390625
- keep_mask: int32 [16384, 256], P(('rows', 'tok')), may hold values from 0 to 1, as said below
- factor_block: float32 [256, 256], replicated, as said below
- factor_trail: bfloat16 [256, 26496], P(None, 'rows'), may hold values from -0.359375 to 0.359375
Outputs:
- pruned: bfloat16 [16384, 256], P(('rows', 'tok'))
- next_input: bfloat16 [128, 16384], replicated
The draws below stay inside these ranges and needn't reach their ends.
Inputs may be any that keep to these rules, and one draw needn't show every extreme that they name: `keep_mask`: in every row, each aligned group of 4 columns holds exactly two ones. `factor_block`: upper triangular, diagonal entries between 0.6 and 1.4.
All inputs are finite; a program needn't handle non-finite values.
Results may differ from the reference program's by a relative error of at most 0.001.
Values may be sent and summed in bfloat16 or wider, within the bound.
No kernel may reach another device: no remote copies, remote signals or barrier semaphores. Data moves between devices by JAX's collectives and lax.ppermute only.
A program may use at most 128 MiB of HBM per device.

```python
import jax
import jax.numpy as jnp
import numpy as np
from jax import lax

OUT = 16384
PANEL = 128
TRAIL = 26496
TOKENS = 128
COLS = 26752


TWO_OF_FOUR = np.array([[1, 1, 0, 0], [1, 0, 1, 0], [1, 0, 0, 1], [0, 1, 1, 0], [0, 1, 0, 1], [0, 0, 1, 1]], dtype=np.int32)


def draw_keep_mask(key, part):
    pattern_ids = jax.random.randint(key, (OUT, 2 * PANEL // 4), 0, 6)
    pattern_table = jnp.asarray(TWO_OF_FOUR)
    return pattern_table[pattern_ids].reshape(OUT, 2 * PANEL).astype(jnp.int32)


def draw_factor_block(key, part):
    span_total = 2 * PANEL
    key_diag = jax.random.fold_in(key, 11)
    key_upper = jax.random.fold_in(key, 12)
    diagonal = jax.random.uniform(key_diag, (span_total,), jnp.float32, 0.6, 1.4)
    spread = 0.06 * jax.random.normal(key_upper, (span_total, span_total), jnp.float32)
    return (jnp.triu(spread, 1) + jnp.diag(diagonal)).astype(jnp.float32)


def level_of(stream_key, dims, split, least, high):
    def one(axis_at, shards_of):
        heights = jax.random.uniform(jax.random.fold_in(jax.random.fold_in(stream_key, 6), axis_at), (shards_of,), jnp.float32, least / len(split), high / len(split))
        return jnp.repeat(jnp.exp(heights), dims[axis_at] // shards_of).reshape((-1,) + (1,) * (len(dims) - axis_at - 1))

    factor_of = one(*split[0])
    for cut in split[1:]:
        factor_of = factor_of * one(*cut)
    return factor_of


def normal_values(own_key, extent, scale, limit, pieces=(), kind=jnp.bfloat16):
    entries = jax.random.normal(own_key, extent, jnp.float32) * scale
    if len(pieces) > 0:
        entries = level_of(own_key, extent, pieces, -0.22, 0.18) * entries
    return jnp.clip(entries, min=-limit, max=limit).astype(kind)


def setup_inputs(seed: int = 0) -> dict:
    keys = jax.random.split(jax.random.key(seed), 7)
    return {
        "calib": normal_values(keys[0], (TOKENS, COLS), 1.0, 6.0, ((0, 2),)),
        "w_panels": normal_values(keys[1], (OUT, 2 * PANEL), COLS ** -0.5, 0.0390625, ((0, 256),)),
        "w_trail": normal_values(keys[2], (OUT, TRAIL), COLS ** -0.5, 0.0390625, ((0, 256),)),
        "keep_mask": draw_keep_mask(jax.random.fold_in(keys[6], 71), 0),
        "factor_block": draw_factor_block(jax.random.fold_in(keys[6], 71), 0),
        "factor_trail": normal_values(keys[5], (2 * PANEL, TRAIL), 0.06, 0.359375, ((1, 128),)),
    }


def sweep_columns(current, keep_part, factor):
    column_count = factor.shape[0]
    errors = jnp.zeros(current.shape, jnp.float32)
    dropped = 1.0 - keep_part.astype(jnp.float32)

    def advance(column, state_pair):
        weights_now, errors_now = state_pair
        col_index = jnp.asarray(column).astype(jnp.int32)
        values = lax.dynamic_index_in_dim(weights_now, col_index, 1, keepdims=False)
        factor_row = lax.dynamic_index_in_dim(factor, col_index, 0, keepdims=False)
        diag_entry = lax.dynamic_index_in_dim(factor_row, col_index, 0, keepdims=False)
        dropping = lax.dynamic_index_in_dim(dropped, col_index, 1, keepdims=False)
        col_error = dropping * values / diag_entry
        weights_now = weights_now - col_error[:, None] * factor_row[None, :]
        errors_now = lax.dynamic_update_slice_in_dim(errors_now, col_error[:, None], col_index, 1)
        return weights_now, errors_now

    return lax.fori_loop(0, column_count, advance, (current, errors))


def reference(calib, w_panels, w_trail, keep_mask, factor_block, factor_trail):
    span_total = factor_block.shape[0]
    current, errors = sweep_columns(w_panels.astype(jnp.float32), keep_mask, factor_block)
    final_weights = current * keep_mask.astype(jnp.float32)
    pruned = final_weights.astype(jnp.bfloat16)
    x_panel = calib[:, :span_total].astype(jnp.float32)
    x_trail = calib[:, span_total:]
    contract = (((1,), (1,)), ((), ()))
    part_panel = lax.dot_general(x_panel, final_weights, contract, precision=lax.Precision.HIGHEST)
    base_trail = lax.dot_general(x_trail, w_trail, contract, preferred_element_type=jnp.float32)
    projected = lax.dot_general(x_trail, factor_trail, contract, preferred_element_type=jnp.float32)
    part_trail = base_trail - lax.dot_general(projected, errors, contract, precision=lax.Precision.HIGHEST)
    next_input = (part_panel + part_trail).astype(jnp.bfloat16)
    return pruned, next_input
```

```python
import functools

import jax
import jax.numpy as jnp
from jax import lax
from jax.experimental import pallas as pl
from jax.experimental.pallas import tpu as pltpu
from jax.sharding import PartitionSpec as P


NY, NX, NZ = 4, 4, 8
CHIPS = NY * NX * NZ
BLOCK = 16
F32 = jnp.float32
BF16 = jnp.bfloat16
VMEM = pl.BlockSpec(memory_space=pltpu.VMEM)
CONTRACT_LAST = (((1,), (1,)), ((), ()))


def chip_id(y, x, z):
    return (y * NX + x) * NZ + z


def coords():
    return [(y, x, z) for y in range(NY) for x in range(NX) for z in range(NZ)]


def row_pairs(bit):
    return [(c, c ^ bit) for c in range(CHIPS)]


def plane_pairs(offset, first):
    pairs = []
    for y, x, z in coords():
        for t in range(2):
            along_x = (t == 0) == first
            peer = chip_id(y, x ^ offset, z) if along_x else chip_id(y ^ offset, x, z)
            pairs.append((chip_id(y, x, z) * 2 + t, peer * 2 + t))
    return pairs


SWAP = [(0, 1), (1, 0)]


def split(v):
    high = v.astype(BF16)
    return high, (v - high.astype(F32)).astype(BF16)


def dot(a, b):
    return jnp.dot(a, b, preferred_element_type=F32)


def sweep_kernel(w_ref, keep_ref, factor_ref, factor_smem, pruned_ref, final_ref, err_ref,
                 wt, scale, keep_t, fh, fl, eh, el, cur, back):
    n = factor_ref.shape[0]
    own = lax.axis_index("tok") * 64
    factor = factor_ref[...]
    eye = (lax.broadcasted_iota(jnp.int32, (n, n), 0) == lax.broadcasted_iota(jnp.int32, (n, n), 1))
    diag = jnp.sum(jnp.where(eye, factor, 0.0), axis=1, keepdims=True)
    ft_high, ft_low = split(factor.T)
    fh[...] = ft_high
    fl[...] = ft_low
    wt[...] = w_ref[...].astype(F32).T
    kept = keep_ref[...].astype(F32).T
    keep_t[...] = kept
    scale[...] = (1.0 - kept) * (1.0 / diag)
    eh[...] = jnp.zeros_like(eh)
    el[...] = jnp.zeros_like(el)
    sub = lax.broadcasted_iota(jnp.int32, (BLOCK, 128), 0)

    def advance(block, carry):
        start = pl.multiple_of(block * BLOCK, BLOCK)
        rows = pl.ds(start, BLOCK)
        high, low = fh[rows, :], fl[rows, :]
        errs_high = eh[...]
        update = dot(high, errs_high) + dot(low, errs_high) + dot(high, el[...])
        cur[...] = wt[rows, :] - update
        cols = [cur[pl.ds(j, 8, stride=0), :] for j in range(BLOCK)]
        errs = jnp.zeros((BLOCK, 128), F32)
        vals = jnp.zeros((BLOCK, 128), F32)
        for j in range(BLOCK):
            e = cols[j] * scale[pl.ds(start + j, 8, stride=0), :]
            for k in range(j + 1, BLOCK):
                cols[k] = cols[k] - e * factor_smem[start + j, start + k]
            wide_e = jnp.concatenate([e] * (BLOCK // 8), axis=0)
            wide_c = jnp.concatenate([cols[j]] * (BLOCK // 8), axis=0)
            errs = jnp.where(sub == j, wide_e, errs)
            vals = jnp.where(sub == j, wide_c, vals)
        err_ref[rows, :] = errs
        final_ref[rows, :] = vals * keep_t[rows, :]
        e_high, e_low = split(errs)
        eh[rows, :] = e_high
        el[rows, :] = e_low
        return carry

    lax.fori_loop(0, n // BLOCK, advance, 0)
    back[...] = final_ref[...].T
    pruned_ref[...] = back[pl.ds(pl.multiple_of(own, 64), 64), :].astype(BF16)


def sweep(w, keep, factor):
    n = factor.shape[0]
    return pl.pallas_call(
        sweep_kernel,
        out_shape=(
            jax.ShapeDtypeStruct((64, n), BF16),
            jax.ShapeDtypeStruct((n, 128), F32),
            jax.ShapeDtypeStruct((n, 128), F32),
        ),
        in_specs=[VMEM, VMEM, VMEM, pl.BlockSpec(memory_space=pltpu.SMEM)],
        out_specs=(VMEM, VMEM, VMEM),
        scratch_shapes=[
            pltpu.VMEM((n, 128), F32),
            pltpu.VMEM((n, 128), F32),
            pltpu.VMEM((n, 128), F32),
            pltpu.VMEM((n, n), BF16),
            pltpu.VMEM((n, n), BF16),
            pltpu.VMEM((n, 128), BF16),
            pltpu.VMEM((n, 128), BF16),
            pltpu.VMEM((BLOCK, 128), F32),
            pltpu.VMEM((128, n), F32),
        ],
        cost_estimate=pl.CostEstimate(flops=10**9, bytes_accessed=20 * 2**20, transcendentals=0),
        name="sweep",
    )(w, keep, factor, factor)


def correct_kernel(base_ref, x_ref, final_ref, proj_ref, err_ref, out_ref):
    x = x_ref[...]
    fin_high, fin_low = split(final_ref[...])
    p_high, p_low = split(proj_ref[...])
    e_high, e_low = split(err_ref[...])
    total = base_ref[...] + (dot(x, fin_high) + dot(x, fin_low))
    total = total - (dot(p_high, e_high) + dot(p_high, e_low) + dot(p_low, e_high))
    out_ref[...] = total.astype(BF16)


def correct(base, x_panel, final, projected, errors):
    return pl.pallas_call(
        correct_kernel,
        out_shape=jax.ShapeDtypeStruct((64, 128), BF16),
        in_specs=[VMEM] * 5,
        out_specs=VMEM,
        cost_estimate=pl.CostEstimate(flops=10**7, bytes_accessed=2**20, transcendentals=0),
        name="correct",
    )(base, x_panel, final, projected, errors)


def place_z_kernel(*refs):
    out_ref = refs[-1]
    z = lax.rem(lax.axis_index("rows"), NZ)
    for o, piece in enumerate(refs[:-1]):
        for k in range(2):
            at = pl.multiple_of((z ^ (2 * o + k)) * 128, 128)
            out_ref[:, pl.ds(at, 128)] = piece[k]


def place_z(pieces):
    return pl.pallas_call(
        place_z_kernel,
        out_shape=jax.ShapeDtypeStruct((64, NZ * 128), BF16),
        in_specs=[VMEM] * len(pieces),
        out_specs=VMEM,
        name="place_z",
    )(*pieces)


def place_all_kernel(*refs):
    pieces, out_ref, sem = refs[:-2], refs[-2], refs[-1]
    chip = lax.axis_index("rows")
    t = lax.axis_index("tok")
    y, x = chip // (NX * NZ), lax.rem(chip // NZ, NX)
    copies = []
    for owner in range(2):
        half = t if owner == 0 else 1 - t
        rows = pl.ds(pl.multiple_of(half * 64, 64), 64)
        for second in range(4):
            for first in range(4):
                x_at = jnp.where(half == 0, x ^ first, x ^ second)
                y_at = jnp.where(half == 0, y ^ second, y ^ first)
                cols = pl.ds(pl.multiple_of((y_at * NX + x_at) * (NZ * 128), NZ * 128), NZ * 128)
                n = len(copies)
                copies.append(
                    pltpu.make_async_copy(
                        pieces[owner * 4 + second].at[first], out_ref.at[rows, cols], sem.at[n]
                    )
                )
                copies[-1].start()
    for copy in copies:
        copy.wait()


def place_all(pieces):
    return pl.pallas_call(
        place_all_kernel,
        out_shape=jax.ShapeDtypeStruct((128, CHIPS * 128), BF16),
        in_specs=[VMEM] * len(pieces),
        out_specs=pl.BlockSpec(memory_space=pl.ANY),
        scratch_shapes=[pltpu.SemaphoreType.DMA((32,))],
        name="place_all",
    )(*pieces)


def gather_output(own):
    both = ("rows", "tok")
    pair = jnp.stack([own, lax.ppermute(own, "rows", row_pairs(1))])
    pieces = [pair] + [lax.ppermute(pair, "rows", row_pairs(o)) for o in (2, 4, 6)]
    line = place_z(pieces)
    block = jnp.stack([line] + [lax.ppermute(line, both, plane_pairs(o, True)) for o in (1, 2, 3)])
    mine = [block] + [lax.ppermute(block, both, plane_pairs(o, False)) for o in (1, 2, 3)]
    other = [lax.ppermute(piece, "tok", SWAP) for piece in mine]
    return place_all(mine + other)


def per_device(calib, w_panels, w_trail, keep_mask, factor_block, factor_trail):
    span = factor_block.shape[0]
    local = factor_trail.shape[1]
    t = lax.axis_index("tok")
    chip = lax.axis_index("rows")

    def ordered(mine, other, axis):
        return jnp.where(
            t == 0,
            jnp.concatenate([mine, other], axis=axis),
            jnp.concatenate([other, mine], axis=axis),
        )

    small = jnp.concatenate([w_panels, keep_mask.astype(BF16)], axis=1)
    small_other = lax.ppermute(small, "tok", SWAP)
    w_other = lax.ppermute(w_trail, "tok", SWAP)

    cols = lax.dynamic_slice_in_dim(calib, span + chip * local, local, 1)
    projected = lax.dot_general(cols, factor_trail, CONTRACT_LAST, preferred_element_type=F32)
    for bit in (1, 2, 4, 8, 16, 32, 64):
        projected = projected + lax.ppermute(projected, "rows", row_pairs(bit))

    panels = ordered(small, small_other, 0)
    pruned, final, errors = sweep(panels[:, :span], panels[:, span:], factor_block)

    x_trail = calib[:, span:]
    base_own = lax.dot_general(x_trail, w_trail, CONTRACT_LAST, preferred_element_type=F32)
    base_other = lax.dot_general(x_trail, w_other, CONTRACT_LAST, preferred_element_type=F32)
    base = ordered(base_own, base_other, 1)
    own = correct(base, calib[:, :span], final, projected, errors)
    return pruned, gather_output(own)


def solution(mesh):
    both = P(("rows", "tok"), None)
    return jax.shard_map(
        per_device,
        mesh=mesh,
        in_specs=(P("tok", None), both, both, both, P(), P(None, "rows")),
        out_specs=(both, P()),
        check_vma=False,
    )
```

```python
import functools

import jax
import jax.numpy as jnp
from jax import lax
from jax.experimental import pallas as pl
from jax.experimental.pallas import tpu as pltpu
from jax.sharding import PartitionSpec as P


NY, NX, NZ = 4, 4, 8
CHIPS = NY * NX * NZ
BLOCK = 16
F32 = jnp.float32
BF16 = jnp.bfloat16
VMEM = pl.BlockSpec(memory_space=pltpu.VMEM)
ANY = pl.BlockSpec(memory_space=pl.ANY)
CONTRACT_LAST = (((1,), (1,)), ((), ()))


def chip_id(y, x, z):
    return (y * NX + x) * NZ + z


def coords():
    return [(y, x, z) for y in range(NY) for x in range(NX) for z in range(NZ)]


def row_pairs(bit):
    return [(c, c ^ bit) for c in range(CHIPS)]


def plane_pairs(offset, first):
    pairs = []
    for y, x, z in coords():
        for t in range(2):
            along_x = (t == 0) == first
            peer = chip_id(y, x ^ offset, z) if along_x else chip_id(y ^ offset, x, z)
            pairs.append((chip_id(y, x, z) * 2 + t, peer * 2 + t))
    return pairs


SWAP = [(0, 1), (1, 0)]


def split(v):
    high = v.astype(BF16)
    return high, (v - high.astype(F32)).astype(BF16)


def dot(a, b):
    return jnp.dot(a, b, preferred_element_type=F32)


def sweep_kernel(w_own, w_other, keep_own, keep_other, factor_ref, calib_ref,
                 pruned_ref, panel_ref, eh, el,
                 w_all, keep_all, x_panel, wt, scale, keep_t, fh, fl, final_t, cur, back, tiles,
                 x_sem, tile_sem):
    n = factor_ref.shape[0]
    blocks = n // BLOCK
    own = pl.multiple_of(lax.axis_index("tok") * 64, 64)
    other = pl.multiple_of(64 - own, 64)

    def tile_copy(block):
        rows = pl.ds(pl.multiple_of(block * BLOCK, BLOCK), BLOCK)
        lanes = pl.ds(pl.multiple_of(block * BLOCK // 128 * 128, 128), 128)
        return pltpu.make_async_copy(
            factor_ref.at[rows, lanes], tiles.at[block], tile_sem.at[block]
        )

    x_copy = pltpu.make_async_copy(calib_ref.at[:, 0:n], x_panel, x_sem)
    x_copy.start()
    for block in range(blocks):
        tile_copy(block).start()
    w_all[pl.ds(own, 64), :] = w_own[...]
    w_all[pl.ds(other, 64), :] = w_other[...]
    keep_all[pl.ds(own, 64), :] = keep_own[...]
    keep_all[pl.ds(other, 64), :] = keep_other[...]
    factor = factor_ref[...]
    eye = (lax.broadcasted_iota(jnp.int32, (n, n), 0) == lax.broadcasted_iota(jnp.int32, (n, n), 1))
    diag = jnp.sum(jnp.where(eye, factor, 0.0), axis=1, keepdims=True)
    ft_high, ft_low = split(factor.T)
    fh[...] = ft_high
    fl[...] = ft_low
    wt[...] = w_all[...].astype(F32).T
    kept = keep_all[...].astype(F32).T
    keep_t[...] = kept
    scale[...] = (1.0 - kept) * (1.0 / diag)
    eh[...] = jnp.zeros_like(eh)
    el[...] = jnp.zeros_like(el)
    sub = lax.broadcasted_iota(jnp.int32, (BLOCK, 128), 0)

    def advance(block, carry):
        start = pl.multiple_of(block * BLOCK, BLOCK)
        lane = lax.rem(start, 128)
        rows = pl.ds(start, BLOCK)
        tile_copy(block).wait()
        high, low = fh[rows, :], fl[rows, :]
        errs_high = eh[...]
        update = dot(high, errs_high) + dot(low, errs_high) + dot(high, el[...])
        cur[...] = wt[rows, :] - update
        cols = [cur[pl.ds(j, 8, stride=0), :] for j in range(BLOCK)]
        errs = jnp.zeros((BLOCK, 128), F32)
        vals = jnp.zeros((BLOCK, 128), F32)
        for j in range(BLOCK):
            e = cols[j] * scale[pl.ds(start + j, 8, stride=0), :]
            for k in range(j + 1, BLOCK):
                cols[k] = cols[k] - e * tiles[block, j, lane + k]
            wide_e = jnp.concatenate([e] * (BLOCK // 8), axis=0)
            wide_c = jnp.concatenate([cols[j]] * (BLOCK // 8), axis=0)
            errs = jnp.where(sub == j, wide_e, errs)
            vals = jnp.where(sub == j, wide_c, vals)
        final_t[rows, :] = vals * keep_t[rows, :]
        e_high, e_low = split(errs)
        eh[rows, :] = e_high
        el[rows, :] = e_low
        return carry

    lax.fori_loop(0, blocks, advance, 0)
    final = final_t[...]
    x_copy.wait()
    fin_high, fin_low = split(final)
    x = x_panel[...]
    panel_ref[...] = dot(x, fin_high) + dot(x, fin_low)
    back[...] = final.T
    pruned_ref[...] = back[pl.ds(own, 64), :].astype(BF16)


def sweep(w_own, w_other, keep_own, keep_other, factor, calib):
    n = factor.shape[0]
    return pl.pallas_call(
        sweep_kernel,
        out_shape=(
            jax.ShapeDtypeStruct((64, n), BF16),
            jax.ShapeDtypeStruct((64, 128), F32),
            jax.ShapeDtypeStruct((n, 128), BF16),
            jax.ShapeDtypeStruct((n, 128), BF16),
        ),
        in_specs=[VMEM] * 5 + [ANY],
        out_specs=(VMEM,) * 4,
        scratch_shapes=[
            pltpu.VMEM((128, n), BF16),
            pltpu.VMEM((128, n), jnp.int32),
            pltpu.VMEM((64, n), BF16),
            pltpu.VMEM((n, 128), F32),
            pltpu.VMEM((n, 128), F32),
            pltpu.VMEM((n, 128), F32),
            pltpu.VMEM((n, n), BF16),
            pltpu.VMEM((n, n), BF16),
            pltpu.VMEM((n, 128), F32),
            pltpu.VMEM((BLOCK, 128), F32),
            pltpu.VMEM((128, n), F32),
            pltpu.SMEM((n // BLOCK, BLOCK, 128), F32),
            pltpu.SemaphoreType.DMA,
            pltpu.SemaphoreType.DMA((n // BLOCK,)),
        ],
        cost_estimate=pl.CostEstimate(flops=10**9, bytes_accessed=20 * 2**20, transcendentals=0),
        name="sweep",
    )(w_own, w_other, keep_own, keep_other, factor, calib)


def base_kernel(calib_ref, own_ref, other_ref, out_ref, x, w, sems):
    parts, width = x.shape[0], x.shape[2]
    first = calib_ref.shape[1] - parts * width
    own = pl.multiple_of(lax.axis_index("tok") * 64, 64)
    other = pl.multiple_of(64 - own, 64)
    copies = []
    for c in range(parts):
        cols = pl.ds(c * width, width)
        copies.append(
            (
                pltpu.make_async_copy(
                    calib_ref.at[:, pl.ds(first + c * width, width)], x.at[c], sems.at[0, c]
                ),
                pltpu.make_async_copy(
                    own_ref.at[:, cols], w.at[c, pl.ds(own, 64), :], sems.at[1, c]
                ),
                pltpu.make_async_copy(
                    other_ref.at[:, cols], w.at[c, pl.ds(other, 64), :], sems.at[2, c]
                ),
            )
        )
        for copy in copies[-1]:
            copy.start()
    total = jnp.zeros(out_ref.shape, F32)
    for c in range(parts):
        for copy in copies[c]:
            copy.wait()
        total = total + lax.dot_general(x[c], w[c], CONTRACT_LAST, preferred_element_type=F32)
    out_ref[...] = total


def base_product(calib, own, other):
    parts = 9
    width = own.shape[1] // parts
    return pl.pallas_call(
        base_kernel,
        out_shape=jax.ShapeDtypeStruct((64, 128), F32),
        in_specs=[ANY] * 3,
        out_specs=VMEM,
        scratch_shapes=[
            pltpu.VMEM((parts, 64, width), BF16),
            pltpu.VMEM((parts, 128, width), BF16),
            pltpu.SemaphoreType.DMA((3, parts)),
        ],
        cost_estimate=pl.CostEstimate(flops=4 * 10**8, bytes_accessed=10 * 2**20, transcendentals=0),
        name="base_product",
    )(calib, own, other)


def correct_kernel(base_ref, panel_ref, proj_ref, eh_ref, el_ref, out_ref):
    p_high, p_low = split(proj_ref[...])
    e_high, e_low = eh_ref[...], el_ref[...]
    fix = dot(p_high, e_high) + dot(p_high, e_low) + dot(p_low, e_high)
    out = ((base_ref[...] + panel_ref[...]) - fix).astype(BF16)
    out_ref[...] = jnp.broadcast_to(out[None], out_ref.shape)


def correct(base, panel, projected, eh, el):
    return pl.pallas_call(
        correct_kernel,
        out_shape=jax.ShapeDtypeStruct((NZ, 64, 128), BF16),
        in_specs=[VMEM] * 5,
        out_specs=VMEM,
        cost_estimate=pl.CostEstimate(flops=10**7, bytes_accessed=2**20, transcendentals=0),
        name="correct",
    )(base, panel, projected, eh, el)


def lay_line_kernel(in_ref, low_ref, high_ref):
    for z in range(NZ):
        low_ref[:, z * 128 : (z + 1) * 128] = in_ref[z, :32, :]
        high_ref[:, z * 128 : (z + 1) * 128] = in_ref[z, 32:, :]


def lay_line(gathered):
    half = jax.ShapeDtypeStruct((32, NZ * 128), BF16)
    return pl.pallas_call(
        lay_line_kernel,
        out_shape=(half, half),
        in_specs=[VMEM],
        out_specs=(VMEM, VMEM),
        name="lay_line",
    )(gathered)


def place_kernel(mine, *refs):
    pieces, out_ref, sem = refs[:8], refs[-2], refs[-1]
    chip = lax.axis_index("rows")
    t = lax.axis_index("tok")
    y, x = chip // (NX * NZ), lax.rem(chip // NZ, NX)
    core = t if mine else 1 - t
    copies = []
    for part in range(2):
        x_first = core == part
        rows = pl.ds(pl.multiple_of(core * 64 + part * 32, 32), 32)
        for second in range(4):
            for first in range(4):
                x_at = jnp.where(x_first, x ^ first, x ^ second)
                y_at = jnp.where(x_first, y ^ second, y ^ first)
                cols = pl.ds(pl.multiple_of((y_at * NX + x_at) * (NZ * 128), NZ * 128), NZ * 128)
                copies.append(
                    pltpu.make_async_copy(
                        pieces[part * 4 + second].at[first], out_ref.at[rows, cols],
                        sem.at[len(copies)],
                    )
                )
                copies[-1].start()
    for copy in copies:
        copy.wait()


def place(mine, pieces, out=None):
    extra = () if out is None else (out,)
    return pl.pallas_call(
        functools.partial(place_kernel, mine),
        out_shape=jax.ShapeDtypeStruct((128, CHIPS * 128), BF16),
        in_specs=[VMEM] * len(pieces) + [ANY] * len(extra),
        out_specs=ANY,
        scratch_shapes=[pltpu.SemaphoreType.DMA((32,))],
        input_output_aliases={} if out is None else {len(pieces): 0},
        cost_estimate=pl.CostEstimate(flops=0, bytes_accessed=8 * 2**20, transcendentals=0),
        name="place_own" if mine else "place_other",
    )(*pieces, *extra)


def gather_output(copies):
    both = ("rows", "tok")
    line = [[chip_id(y, x, z) for z in range(NZ)] for y in range(NY) for x in range(NX)]
    halves = lay_line(lax.all_to_all(copies, "rows", 0, 0, axis_index_groups=line))

    def exchange(value, part, round_one):
        return [
            lax.ppermute(value, both, plane_pairs(o, (part == 0) == round_one)) for o in (1, 2, 3)
        ]

    blocks = [jnp.stack([h] + exchange(h, p, True)) for p, h in enumerate(halves)]
    mine = [piece for p, b in enumerate(blocks) for piece in [b] + exchange(b, p, False)]
    other = [lax.ppermute(piece, "tok", SWAP) for piece in mine]
    return place(False, other, place(True, mine))


def per_device(calib, w_panels, w_trail, keep_mask, factor_block, factor_trail):
    span = factor_block.shape[0]
    local = factor_trail.shape[1]
    chip = lax.axis_index("rows")

    panels_other = lax.ppermute(w_panels, "tok", SWAP)
    keep_other = lax.ppermute(keep_mask, "tok", SWAP)
    w_other = lax.ppermute(w_trail, "tok", SWAP)

    cols = lax.dynamic_slice_in_dim(calib, span + chip * local, local, 1)
    projected = lax.dot_general(cols, factor_trail, CONTRACT_LAST, preferred_element_type=F32)
    for bit in (1, 2, 4, 8, 16, 32, 64):
        projected = projected + lax.ppermute(projected, "rows", row_pairs(bit))

    pruned, panel, eh, el = sweep(
        w_panels, panels_other, keep_mask, keep_other, factor_block, calib
    )
    base = base_product(calib, w_trail, w_other)
    return pruned, gather_output(correct(base, panel, projected, eh, el))


def solution(mesh):
    both = P(("rows", "tok"), None)
    return jax.shard_map(
        per_device,
        mesh=mesh,
        in_specs=(P("tok", None), both, both, both, P(), P(None, "rows")),
        out_specs=(both, P()),
        check_vma=False,
    )
```

```python
import functools

import jax
import jax.numpy as jnp
from jax import lax
from jax.experimental import pallas as pl
from jax.experimental.pallas import tpu as pltpu
from jax.sharding import PartitionSpec as P


NY, NX, NZ = 4, 4, 8
CHIPS = NY * NX * NZ
BLOCK = 16
F32 = jnp.float32
BF16 = jnp.bfloat16
VMEM = pl.BlockSpec(memory_space=pltpu.VMEM)
ANY = pl.BlockSpec(memory_space=pl.ANY)
HBM = pl.BlockSpec(memory_space=pltpu.MemorySpace.HBM)
CONTRACT_LAST = (((1,), (1,)), ((), ()))


def chip_id(y, x, z):
    return (y * NX + x) * NZ + z


def coords():
    return [(y, x, z) for y in range(NY) for x in range(NX) for z in range(NZ)]


def gray(i):
    return i ^ (i >> 1)


def gray_pairs(axis, bit):
    position = {gray(i): i for i in range(NZ)}
    pairs = []
    for here in coords():
        there = list(here)
        there[axis] = position[gray(here[axis]) ^ bit]
        pairs.append((chip_id(*here), chip_id(*there)))
    return pairs


REDUCE_STEPS = ((1, 1), (1, 2), (0, 1), (0, 2), (2, 1), (2, 2), (2, 4))


def plane_pairs(offset, first):
    pairs = []
    for y, x, z in coords():
        for t in range(2):
            along_x = (t == 0) == first
            peer = chip_id(y, x ^ offset, z) if along_x else chip_id(y ^ offset, x, z)
            pairs.append((chip_id(y, x, z) * 2 + t, peer * 2 + t))
    return pairs


SWAP = [(0, 1), (1, 0)]


def params(mib):
    return pltpu.CompilerParams(vmem_limit_bytes=mib * 2**20)


def split(v):
    high = v.astype(BF16)
    return high, (v - high.astype(F32)).astype(BF16)


def dot(a, b):
    return jnp.dot(a, b, preferred_element_type=F32)


def sweep_kernel(w_own, w_other, keep_own, keep_other, factor_ref, calib_ref,
                 pruned_ref, panel_ref, eh, el,
                 w_all, keep_all, factor_all, x_panel, wt, scale, keep_t, fh, fl, final_t, cur, back,
                 tiles, sems, tile_sem):
    n = factor_ref.shape[0]
    blocks = n // BLOCK
    own = pl.multiple_of(lax.axis_index("tok") * 64, 64)
    other = pl.multiple_of(64 - own, 64)

    def tile_copy(block):
        rows = pl.ds(pl.multiple_of(block * BLOCK, BLOCK), BLOCK)
        lanes = pl.ds(pl.multiple_of(block * BLOCK // 128 * 128, 128), 128)
        return pltpu.make_async_copy(
            factor_ref.at[rows, lanes], tiles.at[block], tile_sem.at[block]
        )

    mine, theirs = pl.ds(own, 64), pl.ds(other, 64)
    loads = [
        pltpu.make_async_copy(source, target, sems.at[i])
        for i, (source, target) in enumerate(
            (
                (factor_ref, factor_all),
                (w_own, w_all.at[mine, :]),
                (w_other, w_all.at[theirs, :]),
                (keep_own, keep_all.at[mine, :]),
                (keep_other, keep_all.at[theirs, :]),
                (calib_ref.at[:, 0:n], x_panel),
            )
        )
    ]
    for load in loads:
        load.start()
    for block in range(blocks):
        tile_copy(block).start()
    for load in loads[:-1]:
        load.wait()
    factor = factor_all[...]
    eye = (lax.broadcasted_iota(jnp.int32, (n, n), 0) == lax.broadcasted_iota(jnp.int32, (n, n), 1))
    diag = jnp.sum(jnp.where(eye, factor, 0.0), axis=1, keepdims=True)
    ft_high, ft_low = split(factor.T)
    fh[...] = ft_high
    fl[...] = ft_low
    wt[...] = w_all[...].astype(F32).T
    kept = keep_all[...].astype(F32).T
    keep_t[...] = kept
    scale[...] = (1.0 - kept) * (1.0 / diag)
    eh[...] = jnp.zeros_like(eh)
    el[...] = jnp.zeros_like(el)
    sub = lax.broadcasted_iota(jnp.int32, (BLOCK, 128), 0)

    def advance(block, carry):
        start = pl.multiple_of(block * BLOCK, BLOCK)
        lane = lax.rem(start, 128)
        rows = pl.ds(start, BLOCK)
        tile_copy(block).wait()
        high, low = fh[rows, :], fl[rows, :]
        errs_high = eh[...]
        update = dot(high, errs_high) + dot(low, errs_high) + dot(high, el[...])
        cur[...] = wt[rows, :] - update
        cols = [cur[pl.ds(j, 8, stride=0), :] for j in range(BLOCK)]
        errs = jnp.zeros((BLOCK, 128), F32)
        vals = jnp.zeros((BLOCK, 128), F32)
        for j in range(BLOCK):
            e = cols[j] * scale[pl.ds(start + j, 8, stride=0), :]
            for k in range(j + 1, BLOCK):
                cols[k] = cols[k] - e * tiles[block, j, lane + k]
            wide_e = jnp.concatenate([e] * (BLOCK // 8), axis=0)
            wide_c = jnp.concatenate([cols[j]] * (BLOCK // 8), axis=0)
            errs = jnp.where(sub == j, wide_e, errs)
            vals = jnp.where(sub == j, wide_c, vals)
        final_t[rows, :] = vals * keep_t[rows, :]
        e_high, e_low = split(errs)
        eh[rows, :] = e_high
        el[rows, :] = e_low
        return carry

    lax.fori_loop(0, blocks, advance, 0)
    final = final_t[...]
    loads[-1].wait()
    fin_high, fin_low = split(final)
    x = x_panel[...]
    panel_ref[...] = dot(x, fin_high) + dot(x, fin_low)
    back[...] = final.T
    pruned_ref[...] = back[pl.ds(own, 64), :].astype(BF16)


def sweep(w_own, w_other, keep_own, keep_other, factor, calib):
    n = factor.shape[0]
    return pl.pallas_call(
        sweep_kernel,
        out_shape=(
            jax.ShapeDtypeStruct((64, n), BF16),
            jax.ShapeDtypeStruct((64, 128), F32),
            jax.ShapeDtypeStruct((n, 128), BF16),
            jax.ShapeDtypeStruct((n, 128), BF16),
        ),
        in_specs=[HBM, ANY, HBM, ANY, HBM, HBM],
        out_specs=(VMEM,) * 4,
        scratch_shapes=[
            pltpu.VMEM((128, n), BF16),
            pltpu.VMEM((128, n), jnp.int32),
            pltpu.VMEM((n, n), F32),
            pltpu.VMEM((64, n), BF16),
            pltpu.VMEM((n, 128), F32),
            pltpu.VMEM((n, 128), F32),
            pltpu.VMEM((n, 128), F32),
            pltpu.VMEM((n, n), BF16),
            pltpu.VMEM((n, n), BF16),
            pltpu.VMEM((n, 128), F32),
            pltpu.VMEM((BLOCK, 128), F32),
            pltpu.VMEM((128, n), F32),
            pltpu.SMEM((n // BLOCK, BLOCK, 128), F32),
            pltpu.SemaphoreType.DMA((6,)),
            pltpu.SemaphoreType.DMA((n // BLOCK,)),
        ],
        cost_estimate=pl.CostEstimate(flops=10**9, bytes_accessed=20 * 2**20, transcendentals=0),
        name="sweep",
    )(w_own, w_other, keep_own, keep_other, factor, calib)


def base_kernel(skip, calib_ref, own_ref, other_ref, out_ref, x, w, sems):
    parts, width = x.shape[0], x.shape[2]
    first = calib_ref.shape[1] - own_ref.shape[1]
    own = pl.multiple_of(lax.axis_index("tok") * 64, 64)
    other = pl.multiple_of(64 - own, 64)
    copies = []
    for c in range(parts):
        cols = pl.ds(skip + c * width, width)
        copies.append(
            (
                pltpu.make_async_copy(
                    calib_ref.at[:, pl.ds(first + skip + c * width, width)], x.at[c], sems.at[0, c]
                ),
                pltpu.make_async_copy(
                    own_ref.at[:, cols], w.at[c, pl.ds(own, 64), :], sems.at[1, c]
                ),
                pltpu.make_async_copy(
                    other_ref.at[:, cols], w.at[c, pl.ds(other, 64), :], sems.at[2, c]
                ),
            )
        )
        for copy in copies[-1]:
            copy.start()
    total = jnp.zeros(out_ref.shape, F32)
    for c in range(parts):
        for copy in copies[c]:
            copy.wait()
        total = total + lax.dot_general(x[c], w[c], CONTRACT_LAST, preferred_element_type=F32)
    out_ref[...] = total


def base_product(third, calib, own, other):
    parts = 3
    width = own.shape[1] // (3 * parts)
    return pl.pallas_call(
        functools.partial(base_kernel, third * parts * width),
        out_shape=jax.ShapeDtypeStruct((64, 128), F32),
        in_specs=[ANY, HBM, ANY],
        out_specs=VMEM,
        scratch_shapes=[
            pltpu.VMEM((parts, 64, width), BF16),
            pltpu.VMEM((parts, 128, width), BF16),
            pltpu.SemaphoreType.DMA((3, parts)),
        ],
        cost_estimate=pl.CostEstimate(flops=2 * 10**8, bytes_accessed=8 * 2**20, transcendentals=0),
        compiler_params=params(60),
        name=f"base_product_{third}",
    )(calib, own, other)


def correct_kernel(base_0, base_1, base_2, panel_ref, proj_ref, eh_ref, el_ref, out_ref):
    p_high, p_low = split(proj_ref[...])
    e_high, e_low = eh_ref[...], el_ref[...]
    fix = dot(p_high, e_high) + dot(p_high, e_low) + dot(p_low, e_high)
    base = (base_0[...] + base_1[...]) + (base_2[...] + panel_ref[...])
    out = (base - fix).astype(BF16)
    out_ref[...] = jnp.broadcast_to(out[None], out_ref.shape)


def correct(bases, panel, projected, eh, el):
    return pl.pallas_call(
        correct_kernel,
        out_shape=jax.ShapeDtypeStruct((NZ, 64, 128), BF16),
        in_specs=[VMEM] * 7,
        out_specs=VMEM,
        cost_estimate=pl.CostEstimate(flops=10**7, bytes_accessed=2**20, transcendentals=0),
        compiler_params=params(2),
        name="correct",
    )(*bases, panel, projected, eh, el)


def lay_line_kernel(in_ref, low_ref, high_ref):
    for z in range(NZ):
        low_ref[:, z * 128 : (z + 1) * 128] = in_ref[z, :32, :]
        high_ref[:, z * 128 : (z + 1) * 128] = in_ref[z, 32:, :]


def lay_line(gathered):
    half = jax.ShapeDtypeStruct((32, NZ * 128), BF16)
    return pl.pallas_call(
        lay_line_kernel,
        out_shape=(half, half),
        in_specs=[VMEM],
        out_specs=(VMEM, VMEM),
        compiler_params=params(2),
        name="lay_line",
    )(gathered)


def place_kernel(mine, *refs):
    pieces, out_ref, sem = refs[:8], refs[-2], refs[-1]
    chip = lax.axis_index("rows")
    t = lax.axis_index("tok")
    y, x = chip // (NX * NZ), lax.rem(chip // NZ, NX)
    core = t if mine else 1 - t
    copies = []
    for part in range(2):
        x_first = core == part
        rows = pl.ds(pl.multiple_of(core * 64 + part * 32, 32), 32)
        for second in range(4):
            for first in range(4):
                x_at = jnp.where(x_first, x ^ first, x ^ second)
                y_at = jnp.where(x_first, y ^ second, y ^ first)
                cols = pl.ds(pl.multiple_of((y_at * NX + x_at) * (NZ * 128), NZ * 128), NZ * 128)
                copies.append(
                    pltpu.make_async_copy(
                        pieces[part * 4 + second].at[first], out_ref.at[rows, cols],
                        sem.at[len(copies)],
                    )
                )
                copies[-1].start()
    for copy in copies:
        copy.wait()


def place(mine, pieces, out=None):
    extra = () if out is None else (out,)
    return pl.pallas_call(
        functools.partial(place_kernel, mine),
        out_shape=jax.ShapeDtypeStruct((128, CHIPS * 128), BF16),
        in_specs=[ANY] * (len(pieces) + len(extra)),
        out_specs=ANY,
        scratch_shapes=[pltpu.SemaphoreType.DMA((32,))],
        input_output_aliases={} if out is None else {len(pieces): 0},
        cost_estimate=pl.CostEstimate(flops=0, bytes_accessed=8 * 2**20, transcendentals=0),
        compiler_params=params(1),
        name="place_own" if mine else "place_other",
    )(*pieces, *extra)


def gather_output(copies):
    both = ("rows", "tok")
    line = [[chip_id(y, x, z) for z in range(NZ)] for y in range(NY) for x in range(NX)]
    halves = lay_line(lax.all_to_all(copies, "rows", 0, 0, axis_index_groups=line))

    def exchange(value, part, round_one):
        return [
            lax.ppermute(value, both, plane_pairs(o, (part == 0) == round_one)) for o in (1, 2, 3)
        ]

    blocks = [jnp.stack([h] + exchange(h, p, True)) for p, h in enumerate(halves)]
    mine = [piece for p, b in enumerate(blocks) for piece in [b] + exchange(b, p, False)]
    other = [lax.ppermute(piece, "tok", SWAP) for piece in mine]
    return place(False, other, place(True, mine))


def per_device(calib, w_panels, w_trail, keep_mask, factor_block, factor_trail):
    span = factor_block.shape[0]
    local = factor_trail.shape[1]
    chip = lax.axis_index("rows")

    panels_other = lax.ppermute(w_panels, "tok", SWAP)
    keep_other = lax.ppermute(keep_mask, "tok", SWAP)
    w_other = lax.ppermute(w_trail, "tok", SWAP)

    cols = lax.dynamic_slice_in_dim(calib, span + chip * local, local, 1)
    projected = lax.dot_general(cols, factor_trail, CONTRACT_LAST, preferred_element_type=F32)
    projected, panels_other, keep_other = lax.optimization_barrier(
        (projected, panels_other, keep_other)
    )
    bases = []
    for step, (axis, bit) in enumerate(REDUCE_STEPS):
        received = lax.ppermute(projected, "rows", gray_pairs(axis, bit))
        if step == 0:
            pruned, panel, eh, el = sweep(
                w_panels, panels_other, keep_mask, keep_other, factor_block, calib
            )
            projected, panel, eh, el, w_other = lax.optimization_barrier(
                (projected + received, panel, eh, el, w_other)
            )
        elif step <= 3:
            bases.append(base_product(step - 1, calib, w_trail, w_other))
            projected, bases[-1], w_other = lax.optimization_barrier(
                (projected + received, bases[-1], w_other)
            )
        else:
            projected = projected + received
    return pruned, gather_output(correct(bases, panel, projected, eh, el))


def solution(mesh):
    both = P(("rows", "tok"), None)
    return jax.shard_map(
        per_device,
        mesh=mesh,
        in_specs=(P("tok", None), both, both, both, P(), P(None, "rows")),
        out_specs=(both, P()),
        check_vma=False,
    )
```

```python
import functools

import jax
import jax.numpy as jnp
from jax import lax
from jax.experimental import pallas as pl
from jax.experimental.pallas import tpu as pltpu
from jax.sharding import PartitionSpec as P


NY, NX, NZ = 4, 4, 8
CHIPS = NY * NX * NZ
BLOCK = 16
F32 = jnp.float32
BF16 = jnp.bfloat16
VMEM = pl.BlockSpec(memory_space=pltpu.VMEM)
ANY = pl.BlockSpec(memory_space=pl.ANY)
HBM = pl.BlockSpec(memory_space=pltpu.MemorySpace.HBM)
CONTRACT_LAST = (((1,), (1,)), ((), ()))


def chip_id(y, x, z):
    return (y * NX + x) * NZ + z


def coords():
    return [(y, x, z) for y in range(NY) for x in range(NX) for z in range(NZ)]


def gray(i):
    return i ^ (i >> 1)


def gray_pairs(axis, bit):
    position = {gray(i): i for i in range(NZ)}
    pairs = []
    for here in coords():
        there = list(here)
        there[axis] = position[gray(here[axis]) ^ bit]
        pairs.append((chip_id(*here), chip_id(*there)))
    return pairs


REDUCE_STEPS = ((1, 1), (1, 2), (0, 1), (0, 2), (2, 1), (2, 2), (2, 4))


def plane_pairs(offset, first):
    pairs = []
    for y, x, z in coords():
        for t in range(2):
            along_x = (t == 0) == first
            peer = chip_id(y, x ^ offset, z) if along_x else chip_id(y ^ offset, x, z)
            pairs.append((chip_id(y, x, z) * 2 + t, peer * 2 + t))
    return pairs


SWAP = [(0, 1), (1, 0)]
ORDER = (3, 2, 1)


def params(mib):
    return pltpu.CompilerParams(vmem_limit_bytes=mib * 2**20)


def split(v):
    high = v.astype(BF16)
    return high, (v - high.astype(F32)).astype(BF16)


def dot(a, b):
    return jnp.dot(a, b, preferred_element_type=F32)


def prepare_kernel(w_own, w_other, keep_own, keep_other, factor_ref,
                   tiles, wt, scale, keep_t, fh, fl, w_all, keep_all):
    n = factor_ref.shape[0]
    own = pl.multiple_of(lax.axis_index("tok") * 64, 64)
    other = pl.multiple_of(64 - own, 64)
    w_all[pl.ds(own, 64), :] = w_own[...]
    w_all[pl.ds(other, 64), :] = w_other[...]
    keep_all[pl.ds(own, 64), :] = keep_own[...]
    keep_all[pl.ds(other, 64), :] = keep_other[...]
    factor = factor_ref[...]
    for block in range(n // BLOCK):
        rows, lanes = block * BLOCK, block * BLOCK // 128 * 128
        tiles[block] = factor_ref[rows : rows + BLOCK, lanes : lanes + 128]
    eye = (lax.broadcasted_iota(jnp.int32, (n, n), 0) == lax.broadcasted_iota(jnp.int32, (n, n), 1))
    diag = jnp.sum(jnp.where(eye, factor, 0.0), axis=1, keepdims=True)
    ft_high, ft_low = split(factor.T)
    fh[...] = ft_high
    fl[...] = ft_low
    wt[...] = w_all[...].astype(F32).T
    kept = keep_all[...].astype(F32).T
    keep_t[...] = kept
    scale[...] = (1.0 - kept) * (1.0 / diag)


def prepare(w_own, w_other, keep_own, keep_other, factor):
    n = factor.shape[0]
    tall = jax.ShapeDtypeStruct((n, 128), F32)
    square = jax.ShapeDtypeStruct((n, n), BF16)
    tiles = jax.ShapeDtypeStruct((n // BLOCK, BLOCK, 128), F32)
    return pl.pallas_call(
        prepare_kernel,
        out_shape=(tiles, tall, tall, tall, square, square),
        in_specs=[VMEM] * 5,
        out_specs=(VMEM,) * 6,
        scratch_shapes=[pltpu.VMEM((128, n), BF16), pltpu.VMEM((128, n), jnp.int32)],
        cost_estimate=pl.CostEstimate(flops=10**8, bytes_accessed=6 * 2**20, transcendentals=0),
        compiler_params=params(8),
        name="prepare",
    )(w_own, w_other, keep_own, keep_other, factor)


def sweep_blocks(first, count, tiles_ref, wt, scale, keep_t, fh, fl, eh, el, final_t, cur, tiles,
                 tile_sem):
    sub = lax.broadcasted_iota(jnp.int32, (BLOCK, 128), 0)

    def tile_copy(block):
        return pltpu.make_async_copy(
            tiles_ref.at[block], tiles.at[block - first], tile_sem.at[block - first]
        )

    for block in range(first, first + count):
        tile_copy(block).start()

    def advance(block, carry):
        start = pl.multiple_of(block * BLOCK, BLOCK)
        lane = lax.rem(start, 128)
        rows = pl.ds(start, BLOCK)
        tile_copy(block).wait()
        high, low = fh[rows, :], fl[rows, :]
        errs_high = eh[...]
        update = dot(high, errs_high) + dot(low, errs_high) + dot(high, el[...])
        cur[...] = wt[rows, :] - update
        cols = [cur[pl.ds(j, 8, stride=0), :] for j in range(BLOCK)]
        errs = jnp.zeros((BLOCK, 128), F32)
        vals = jnp.zeros((BLOCK, 128), F32)
        for j in range(BLOCK):
            e = cols[j] * scale[pl.ds(start + j, 8, stride=0), :]
            for k in range(j + 1, BLOCK):
                cols[k] = cols[k] - e * tiles[block - first, j, lane + k]
            wide_e = jnp.concatenate([e] * (BLOCK // 8), axis=0)
            wide_c = jnp.concatenate([cols[j]] * (BLOCK // 8), axis=0)
            errs = jnp.where(sub == j, wide_e, errs)
            vals = jnp.where(sub == j, wide_c, vals)
        final_t[rows, :] = vals * keep_t[rows, :]
        e_high, e_low = split(errs)
        eh[rows, :] = e_high
        el[rows, :] = e_low
        return carry

    lax.fori_loop(first, first + count, advance, 0)


def sweep_first_kernel(tiles_ref, wt, scale, keep_t, fh, fl, eh, el, final_t, cur, tiles, sem):
    eh[...] = jnp.zeros_like(eh)
    el[...] = jnp.zeros_like(el)
    final_t[...] = jnp.zeros_like(final_t)
    count = tiles_ref.shape[0] // 2
    sweep_blocks(0, count, tiles_ref, wt, scale, keep_t, fh, fl, eh, el, final_t, cur, tiles, sem)


def sweep_second_kernel(tiles_ref, wt, scale, keep_t, fh, fl, eh_in, el_in, final_in,
                        eh, el, fin_high, fin_low, pruned_ref, final_t, back, cur, tiles, sem):
    own = pl.multiple_of(lax.axis_index("tok") * 64, 64)
    eh[...] = eh_in[...]
    el[...] = el_in[...]
    final_t[...] = final_in[...]
    count = tiles_ref.shape[0] // 2
    sweep_blocks(count, count, tiles_ref, wt, scale, keep_t, fh, fl, eh, el, final_t, cur, tiles,
                 sem)
    final = final_t[...]
    high, low = split(final)
    fin_high[...] = high
    fin_low[...] = low
    back[...] = final.T
    pruned_ref[...] = back[pl.ds(own, 64), :].astype(BF16)


def sweep_scratch(n):
    half = n // BLOCK // 2
    return [
        pltpu.VMEM((BLOCK, 128), F32),
        pltpu.SMEM((half, BLOCK, 128), F32),
        pltpu.SemaphoreType.DMA((half,)),
    ]


def sweep_first(prepared):
    n = prepared[0].shape[0] * BLOCK
    narrow = jax.ShapeDtypeStruct((n, 128), BF16)
    return pl.pallas_call(
        sweep_first_kernel,
        out_shape=(narrow, narrow, jax.ShapeDtypeStruct((n, 128), F32)),
        in_specs=[VMEM] * 6,
        out_specs=(VMEM,) * 3,
        scratch_shapes=sweep_scratch(n),
        cost_estimate=pl.CostEstimate(flops=10**8, bytes_accessed=8 * 2**20, transcendentals=0),
        compiler_params=params(8),
        name="sweep_first",
    )(*prepared)


def sweep_second(prepared, state):
    n = prepared[0].shape[0] * BLOCK
    narrow = jax.ShapeDtypeStruct((n, 128), BF16)
    return pl.pallas_call(
        sweep_second_kernel,
        out_shape=(narrow,) * 4 + (jax.ShapeDtypeStruct((64, n), BF16),),
        in_specs=[VMEM] * 9,
        out_specs=(VMEM,) * 5,
        scratch_shapes=[pltpu.VMEM((n, 128), F32), pltpu.VMEM((128, n), F32)] + sweep_scratch(n),
        cost_estimate=pl.CostEstimate(flops=10**8, bytes_accessed=8 * 2**20, transcendentals=0),
        compiler_params=params(8),
        name="sweep_second",
    )(*prepared, *state)


def base_kernel(skip, calib_ref, own_ref, other_ref, out_ref, x, w, sems):
    parts, width = x.shape[0], x.shape[2]
    first = calib_ref.shape[1] - own_ref.shape[1]
    own = pl.multiple_of(lax.axis_index("tok") * 64, 64)
    other = pl.multiple_of(64 - own, 64)
    copies = []
    for c in range(parts):
        cols = pl.ds(skip + c * width, width)
        copies.append(
            (
                pltpu.make_async_copy(
                    calib_ref.at[:, pl.ds(first + skip + c * width, width)], x.at[c], sems.at[0, c]
                ),
                pltpu.make_async_copy(
                    own_ref.at[:, cols], w.at[c, pl.ds(own, 64), :], sems.at[1, c]
                ),
                pltpu.make_async_copy(
                    other_ref.at[:, cols], w.at[c, pl.ds(other, 64), :], sems.at[2, c]
                ),
            )
        )
        for copy in copies[-1]:
            copy.start()
    total = jnp.zeros(out_ref.shape, F32)
    for c in range(parts):
        for copy in copies[c]:
            copy.wait()
        total = total + lax.dot_general(x[c], w[c], CONTRACT_LAST, preferred_element_type=F32)
    out_ref[...] = total


CHUNK = 9 * 128


def base_product(part, calib, own, other):
    chunks = own.shape[1] // CHUNK
    begin, end = part * chunks // 4, (part + 1) * chunks // 4
    parts = end - begin
    return pl.pallas_call(
        functools.partial(base_kernel, begin * CHUNK),
        out_shape=jax.ShapeDtypeStruct((64, 128), F32),
        in_specs=[HBM, HBM, ANY],
        out_specs=VMEM,
        scratch_shapes=[
            pltpu.VMEM((parts, 64, CHUNK), BF16),
            pltpu.VMEM((parts, 128, CHUNK), BF16),
            pltpu.SemaphoreType.DMA((3, parts)),
        ],
        cost_estimate=pl.CostEstimate(flops=10**8, bytes_accessed=8 * 2**20, transcendentals=0),
        compiler_params=params(58),
        name=f"base_product_{part}",
    )(calib, own, other)


def correct_kernel(base_0, base_1, base_2, base_3, x_ref, proj_ref, eh_ref, el_ref, fh_ref, fl_ref,
                   out_ref):
    p_high, p_low = split(proj_ref[...])
    e_high, e_low = eh_ref[...], el_ref[...]
    x = x_ref[...]
    base = (base_0[...] + base_1[...]) + (base_2[...] + base_3[...])
    base = base + (dot(x, fh_ref[...]) + dot(x, fl_ref[...]))
    fix = dot(p_high, e_high) + dot(p_high, e_low) + dot(p_low, e_high)
    out = (base - fix).astype(BF16)
    out_ref[...] = jnp.broadcast_to(out[None], out_ref.shape)


def correct(bases, x_panel, projected, swept):
    return pl.pallas_call(
        correct_kernel,
        out_shape=jax.ShapeDtypeStruct((NZ, 64, 128), BF16),
        in_specs=[VMEM] * 10,
        out_specs=VMEM,
        cost_estimate=pl.CostEstimate(flops=10**7, bytes_accessed=2**20, transcendentals=0),
        compiler_params=params(4),
        name="correct",
    )(*bases, x_panel, projected, *swept)


def lay_line_kernel(in_ref, low_ref, high_ref):
    for z in range(NZ):
        low_ref[:, z * 128 : (z + 1) * 128] = in_ref[z, :32, :]
        high_ref[:, z * 128 : (z + 1) * 128] = in_ref[z, 32:, :]


def lay_line(gathered):
    half = jax.ShapeDtypeStruct((32, NZ * 128), BF16)
    return pl.pallas_call(
        lay_line_kernel,
        out_shape=(half, half),
        in_specs=[VMEM],
        out_specs=(VMEM, VMEM),
        compiler_params=params(2),
        name="lay_line",
    )(gathered)


def place_kernel(mine, second, *refs):
    pieces, out_ref, sem = refs[:2], refs[-2], refs[-1]
    chip = lax.axis_index("rows")
    t = lax.axis_index("tok")
    y, x = chip // (NX * NZ), lax.rem(chip // NZ, NX)
    core = t if mine else 1 - t
    copies = []
    for part in range(2):
        x_first = core == part
        rows = pl.ds(pl.multiple_of(core * 64 + part * 32, 32), 32)
        for first in range(4):
            x_at = jnp.where(x_first, x ^ first, x ^ second)
            y_at = jnp.where(x_first, y ^ second, y ^ first)
            cols = pl.ds(pl.multiple_of((y_at * NX + x_at) * (NZ * 128), NZ * 128), NZ * 128)
            copies.append(
                pltpu.make_async_copy(
                    pieces[part].at[first], out_ref.at[rows, cols], sem.at[len(copies)]
                )
            )
            copies[-1].start()
    for copy in copies:
        copy.wait()


def place(mine, second, pieces, out):
    extra = () if out is None else (out,)
    return pl.pallas_call(
        functools.partial(place_kernel, mine, second),
        out_shape=jax.ShapeDtypeStruct((128, CHIPS * 128), BF16),
        in_specs=[ANY] * (2 + len(extra)),
        out_specs=ANY,
        scratch_shapes=[pltpu.SemaphoreType.DMA((8,))],
        input_output_aliases={} if out is None else {2: 0},
        cost_estimate=pl.CostEstimate(flops=0, bytes_accessed=2**20, transcendentals=0),
        compiler_params=params(1),
        name=f"place_{'own' if mine else 'other'}_{second}",
    )(*pieces, *extra)


def gather_output(copies):
    both = ("rows", "tok")
    line = [[chip_id(y, x, z) for z in range(NZ)] for y in range(NY) for x in range(NX)]
    halves = lay_line(lax.all_to_all(copies, "rows", 0, 0, axis_index_groups=line))

    def exchange(value, part, round_one, offset):
        return lax.ppermute(value, both, plane_pairs(offset, (part == 0) == round_one))

    blocks = [
        jnp.stack([h] + [exchange(h, p, True, o) for o in (1, 2, 3)]) for p, h in enumerate(halves)
    ]
    mine = {0: blocks}
    for o in ORDER:
        mine[o] = [exchange(b, p, False, o) for p, b in enumerate(blocks)]
    def swap(o):
        return [lax.ppermute(v, "tok", SWAP) for v in mine[o]]

    early, middle, last = ORDER
    other = {o: swap(o) for o in (0, early, middle)}
    out = place(True, 0, mine[0], None)
    out = place(True, early, mine[early], out)
    out = place(False, 0, other[0], out)
    out, *mine[last] = lax.optimization_barrier((out, *mine[last]))
    other[last] = swap(last)
    out = place(True, middle, mine[middle], out)
    out = place(False, early, other[early], out)
    out = place(False, middle, other[middle], out)
    out = place(True, last, mine[last], out)
    return place(False, last, other[last], out)


def per_device(calib, w_panels, w_trail, keep_mask, factor_block, factor_trail):
    span = factor_block.shape[0]
    local = factor_trail.shape[1]
    chip = lax.axis_index("rows")

    panels_other = lax.ppermute(w_panels, "tok", SWAP)
    keep_other = lax.ppermute(keep_mask, "tok", SWAP)
    cols = lax.dynamic_slice_in_dim(calib, span + chip * local, local, 1)
    projected = lax.dot_general(cols, factor_trail, CONTRACT_LAST, preferred_element_type=F32)
    x_panel = calib[:, :span]
    tie = lax.optimization_barrier
    projected, panels_other, keep_other, w_sent = tie(
        (projected, panels_other, keep_other, w_trail)
    )
    w_other = lax.ppermute(w_sent, "tok", SWAP)
    bases = []
    for step, (axis, bit) in enumerate(REDUCE_STEPS):
        received = lax.ppermute(projected, "rows", gray_pairs(axis, bit))
        if step == 0:
            prepared = prepare(w_panels, panels_other, keep_mask, keep_other, factor_block)
            projected, *prepared = tie((projected + received, *prepared))
        elif step == 1:
            state = sweep_first(prepared)
            projected, w_other, x_panel, *state = tie(
                (projected + received, w_other, x_panel, *state)
            )
        elif step <= 5:
            base = base_product(step - 2, calib, w_trail, w_other)
            projected, w_other, base = tie((projected + received, w_other, base))
            bases.append(base)
        else:
            *swept, pruned = sweep_second(prepared, state)
            projected = projected + received
    return pruned, gather_output(correct(bases, x_panel, projected, swept))


def solution(mesh):
    both = P(("rows", "tok"), None)
    return jax.shard_map(
        per_device,
        mesh=mesh,
        in_specs=(P("tok", None), both, both, both, P(), P(None, "rows")),
        out_specs=(both, P()),
        check_vma=False,
    )
```

```python
import functools

import jax
import jax.numpy as jnp
from jax import lax
from jax.experimental import pallas as pl
from jax.experimental.pallas import tpu as pltpu
from jax.sharding import PartitionSpec as P


NY, NX, NZ = 4, 4, 8
CHIPS = NY * NX * NZ
BLOCK = 16
F32 = jnp.float32
BF16 = jnp.bfloat16
VMEM = pl.BlockSpec(memory_space=pltpu.VMEM)
ANY = pl.BlockSpec(memory_space=pl.ANY)
HBM = pl.BlockSpec(memory_space=pltpu.MemorySpace.HBM)
CONTRACT_LAST = (((1,), (1,)), ((), ()))


def chip_id(y, x, z):
    return (y * NX + x) * NZ + z


def coords():
    return [(y, x, z) for y in range(NY) for x in range(NX) for z in range(NZ)]


def gray(i):
    return i ^ (i >> 1)


def gray_pairs(axis, bit):
    position = {gray(i): i for i in range(NZ)}
    pairs = []
    for here in coords():
        there = list(here)
        there[axis] = position[gray(here[axis]) ^ bit]
        pairs.append((chip_id(*here), chip_id(*there)))
    return pairs


REDUCE_STEPS = ((1, 1), (1, 2), (0, 1), (0, 2), (2, 1), (2, 2), (2, 4))


def plane_pairs(offset, first):
    pairs = []
    for y, x, z in coords():
        for t in range(2):
            along_x = (t == 0) == first
            peer = chip_id(y, x ^ offset, z) if along_x else chip_id(y ^ offset, x, z)
            pairs.append((chip_id(y, x, z) * 2 + t, peer * 2 + t))
    return pairs


SWAP = [(0, 1), (1, 0)]


def params(mib):
    return pltpu.CompilerParams(vmem_limit_bytes=mib * 2**20)


def split(v):
    high = v.astype(BF16)
    return high, (v - high.astype(F32)).astype(BF16)


def in_hbm(array):
    return pltpu.with_memory_space_constraint(array, pltpu.MemorySpace.HBM)


def dot(a, b):
    return jnp.dot(a, b, preferred_element_type=F32)


def prepare_kernel(w_own, w_other, keep_own, keep_other, factor_ref,
                   tiles, wt, scale, keep_t, fh, fl, w_all, keep_all, factor_all, sems):
    n = factor_ref.shape[0]
    own = pl.multiple_of(lax.axis_index("tok") * 64, 64)
    other = pl.multiple_of(64 - own, 64)
    loads = [
        pltpu.make_async_copy(factor_ref, factor_all, sems.at[0]),
        pltpu.make_async_copy(w_own, w_all.at[pl.ds(own, 64), :], sems.at[1]),
        pltpu.make_async_copy(keep_own, keep_all.at[pl.ds(own, 64), :], sems.at[2]),
    ]
    for load in loads:
        load.start()
    w_all[pl.ds(other, 64), :] = w_other[...]
    keep_all[pl.ds(other, 64), :] = keep_other[...]
    for load in loads:
        load.wait()
    factor = factor_all[...]
    for block in range(n // BLOCK):
        rows, lanes = block * BLOCK, block * BLOCK // 128 * 128
        tiles[block] = factor_all[rows : rows + BLOCK, lanes : lanes + 128]
    eye = (lax.broadcasted_iota(jnp.int32, (n, n), 0) == lax.broadcasted_iota(jnp.int32, (n, n), 1))
    diag = jnp.sum(jnp.where(eye, factor, 0.0), axis=1, keepdims=True)
    ft_high, ft_low = split(factor.T)
    fh[...] = ft_high
    fl[...] = ft_low
    wt[...] = w_all[...].astype(F32).T
    kept = keep_all[...].astype(F32).T
    keep_t[...] = kept
    scale[...] = (1.0 - kept) * (1.0 / diag)


def prepare(w_own, w_other, keep_own, keep_other, factor):
    n = factor.shape[0]
    tall = jax.ShapeDtypeStruct((n, 128), F32)
    square = jax.ShapeDtypeStruct((n, n), BF16)
    tiles = jax.ShapeDtypeStruct((n // BLOCK, BLOCK, 128), F32)
    return pl.pallas_call(
        prepare_kernel,
        out_shape=(tiles, tall, tall, tall, square, square),
        in_specs=[HBM, VMEM, HBM, VMEM, HBM],
        out_specs=(VMEM,) * 6,
        scratch_shapes=[
            pltpu.VMEM((128, n), BF16),
            pltpu.VMEM((128, n), jnp.int32),
            pltpu.VMEM((n, n), F32),
            pltpu.SemaphoreType.DMA((3,)),
        ],
        cost_estimate=pl.CostEstimate(flops=10**8, bytes_accessed=6 * 2**20, transcendentals=0),
        compiler_params=params(4),
        name="prepare",
    )(in_hbm(w_own), w_other, in_hbm(keep_own), keep_other, in_hbm(factor))


def sweep_blocks(first, count, tiles_ref, wt, scale, keep_t, fh, fl, eh, el, final_t, cur, tiles,
                 tile_sem):
    sub = lax.broadcasted_iota(jnp.int32, (BLOCK, 128), 0)

    def tile_copy(block):
        return pltpu.make_async_copy(
            tiles_ref.at[block], tiles.at[block - first], tile_sem.at[block - first]
        )

    for block in range(first, first + count):
        tile_copy(block).start()

    def advance(block, carry):
        start = pl.multiple_of(block * BLOCK, BLOCK)
        lane = lax.rem(start, 128)
        rows = pl.ds(start, BLOCK)
        tile_copy(block).wait()
        high, low = fh[rows, :], fl[rows, :]
        errs_high = eh[...]
        update = dot(high, errs_high) + dot(low, errs_high) + dot(high, el[...])
        cur[...] = wt[rows, :] - update
        cols = [cur[pl.ds(j, 8, stride=0), :] for j in range(BLOCK)]
        errs = jnp.zeros((BLOCK, 128), F32)
        vals = jnp.zeros((BLOCK, 128), F32)
        for j in range(BLOCK):
            e = cols[j] * scale[pl.ds(start + j, 8, stride=0), :]
            for k in range(j + 1, BLOCK):
                cols[k] = cols[k] - e * tiles[block - first, j, lane + k]
            wide_e = jnp.concatenate([e] * (BLOCK // 8), axis=0)
            wide_c = jnp.concatenate([cols[j]] * (BLOCK // 8), axis=0)
            errs = jnp.where(sub == j, wide_e, errs)
            vals = jnp.where(sub == j, wide_c, vals)
        final_t[rows, :] = vals * keep_t[rows, :]
        e_high, e_low = split(errs)
        eh[rows, :] = e_high
        el[rows, :] = e_low
        return carry

    lax.fori_loop(first, first + count, advance, 0)


def sweep_first_kernel(tiles_ref, wt, scale, keep_t, fh, fl, calib_ref, eh, el, final_t, x_out,
                       cur, tiles, sem, load_sem):
    load = pltpu.make_async_copy(calib_ref, x_out, load_sem)
    load.start()
    eh[...] = jnp.zeros_like(eh)
    el[...] = jnp.zeros_like(el)
    final_t[...] = jnp.zeros_like(final_t)
    count = tiles_ref.shape[0] // 2
    sweep_blocks(0, count, tiles_ref, wt, scale, keep_t, fh, fl, eh, el, final_t, cur, tiles, sem)
    load.wait()


def sweep_second_kernel(tiles_ref, wt, scale, keep_t, fh, fl, eh_in, el_in, final_in, trail_ref,
                        eh, el, fin_high, fin_low, pruned_ref, trail_out,
                        final_t, back, cur, tiles, sem, load_sem):
    load = pltpu.make_async_copy(trail_ref, trail_out, load_sem)
    load.start()
    own = pl.multiple_of(lax.axis_index("tok") * 64, 64)
    eh[...] = eh_in[...]
    el[...] = el_in[...]
    final_t[...] = final_in[...]
    count = tiles_ref.shape[0] // 2
    sweep_blocks(count, count, tiles_ref, wt, scale, keep_t, fh, fl, eh, el, final_t, cur, tiles,
                 sem)
    final = final_t[...]
    high, low = split(final)
    fin_high[...] = high
    fin_low[...] = low
    back[...] = final.T
    pruned_ref[...] = back[pl.ds(own, 64), :].astype(BF16)
    load.wait()


def sweep_scratch(n):
    half = n // BLOCK // 2
    return [
        pltpu.VMEM((BLOCK, 128), F32),
        pltpu.SMEM((half, BLOCK, 128), F32),
        pltpu.SemaphoreType.DMA((half,)),
        pltpu.SemaphoreType.DMA,
    ]


def sweep_first(prepared, calib):
    n = prepared[0].shape[0] * BLOCK
    narrow = jax.ShapeDtypeStruct((n, 128), BF16)
    return pl.pallas_call(
        sweep_first_kernel,
        out_shape=(
            narrow, narrow, jax.ShapeDtypeStruct((n, 128), F32),
            jax.ShapeDtypeStruct(calib.shape, BF16),
        ),
        in_specs=[VMEM] * 6 + [HBM],
        out_specs=(VMEM,) * 4,
        scratch_shapes=sweep_scratch(n),
        cost_estimate=pl.CostEstimate(flops=10**8, bytes_accessed=8 * 2**20, transcendentals=0),
        compiler_params=params(10),
        name="sweep_first",
    )(*prepared, in_hbm(calib))


def sweep_second(prepared, state, w_trail):
    n = prepared[0].shape[0] * BLOCK
    narrow = jax.ShapeDtypeStruct((n, 128), BF16)
    return pl.pallas_call(
        sweep_second_kernel,
        out_shape=(narrow,) * 4
        + (jax.ShapeDtypeStruct((64, n), BF16), jax.ShapeDtypeStruct(w_trail.shape, BF16)),
        in_specs=[VMEM] * 9 + [HBM],
        out_specs=(VMEM,) * 6,
        scratch_shapes=[pltpu.VMEM((n, 128), F32), pltpu.VMEM((128, n), F32)] + sweep_scratch(n),
        cost_estimate=pl.CostEstimate(flops=10**8, bytes_accessed=8 * 2**20, transcendentals=0),
        compiler_params=params(10),
        name="sweep_second",
    )(*prepared, *state, in_hbm(w_trail))


def base_kernel(begin, width, x_ref, own_ref, other_ref, out_ref):
    skip = x_ref.shape[1] - own_ref.shape[1]
    mine = jnp.zeros((64, 64), F32)
    theirs = jnp.zeros((64, 64), F32)
    for at in range(begin, begin + width, CHUNK):
        x = x_ref[:, skip + at : skip + at + CHUNK]
        cols = slice(at, at + CHUNK)
        mine = mine + lax.dot_general(
            x, own_ref[:, cols], CONTRACT_LAST, preferred_element_type=F32
        )
        theirs = theirs + lax.dot_general(
            x, other_ref[:, cols], CONTRACT_LAST, preferred_element_type=F32
        )
    out_ref[0] = mine
    out_ref[1] = theirs


CHUNK = 9 * 128


def base_product(part, x, own, other):
    chunks = own.shape[1] // CHUNK
    begin, end = part * chunks // 2, (part + 1) * chunks // 2
    return pl.pallas_call(
        functools.partial(base_kernel, begin * CHUNK, (end - begin) * CHUNK),
        out_shape=jax.ShapeDtypeStruct((2, 64, 64), F32),
        in_specs=[VMEM] * 3,
        out_specs=VMEM,
        cost_estimate=pl.CostEstimate(flops=10**8, bytes_accessed=8 * 2**20, transcendentals=0),
        compiler_params=params(4),
        name=f"base_product_{part}",
    )(x, own, other)


def correct_kernel(base_0, base_1, x_ref, proj_ref, eh_ref, el_ref, fh_ref, fl_ref,
                   out_ref):
    p_high, p_low = split(proj_ref[...])
    e_high, e_low = eh_ref[...], el_ref[...]
    x = x_ref[:, : eh_ref.shape[0]]
    mine = base_0[0] + base_1[0]
    theirs = base_0[1] + base_1[1]
    first = lax.axis_index("tok") == 0
    base = jnp.concatenate(
        [jnp.where(first, mine, theirs), jnp.where(first, theirs, mine)], axis=1
    )
    base = base + (dot(x, fh_ref[...]) + dot(x, fl_ref[...]))
    fix = dot(p_high, e_high) + dot(p_high, e_low) + dot(p_low, e_high)
    out = (base - fix).astype(BF16)
    out_ref[...] = jnp.broadcast_to(out[None], out_ref.shape)


def correct(bases, x_all, projected, swept):
    return pl.pallas_call(
        correct_kernel,
        out_shape=jax.ShapeDtypeStruct((NZ, 64, 128), BF16),
        in_specs=[VMEM] * 8,
        out_specs=VMEM,
        cost_estimate=pl.CostEstimate(flops=10**7, bytes_accessed=2**20, transcendentals=0),
        compiler_params=params(4),
        name="correct",
    )(*bases, x_all, projected, *swept)


def lay_line_kernel(in_ref, low_ref, high_ref):
    for z in range(NZ):
        low_ref[:, z * 128 : (z + 1) * 128] = in_ref[z, :32, :]
        high_ref[:, z * 128 : (z + 1) * 128] = in_ref[z, 32:, :]


def lay_line(gathered):
    half = jax.ShapeDtypeStruct((32, NZ * 128), BF16)
    return pl.pallas_call(
        lay_line_kernel,
        out_shape=(half, half),
        in_specs=[VMEM],
        out_specs=(VMEM, VMEM),
        compiler_params=params(2),
        name="lay_line",
    )(gathered)


def place_kernel(mine, *refs):
    pieces, out_ref, sem = refs[:8], refs[-2], refs[-1]
    chip = lax.axis_index("rows")
    t = lax.axis_index("tok")
    y, x = chip // (NX * NZ), lax.rem(chip // NZ, NX)
    core = t if mine else 1 - t
    copies = []
    for part in range(2):
        x_first = core == part
        rows = pl.ds(pl.multiple_of(core * 64 + part * 32, 32), 32)
        for second in range(4):
            for first in range(4):
                x_at = jnp.where(x_first, x ^ first, x ^ second)
                y_at = jnp.where(x_first, y ^ second, y ^ first)
                cols = pl.ds(pl.multiple_of((y_at * NX + x_at) * (NZ * 128), NZ * 128), NZ * 128)
                copies.append(
                    pltpu.make_async_copy(
                        pieces[part * 4 + second].at[first], out_ref.at[rows, cols],
                        sem.at[len(copies)],
                    )
                )
                copies[-1].start()
    for copy in copies:
        copy.wait()


def place(mine, pieces, out=None):
    extra = () if out is None else (out,)
    return pl.pallas_call(
        functools.partial(place_kernel, mine),
        out_shape=jax.ShapeDtypeStruct((128, CHIPS * 128), BF16),
        in_specs=[ANY] * (len(pieces) + len(extra)),
        out_specs=ANY,
        scratch_shapes=[pltpu.SemaphoreType.DMA((32,))],
        input_output_aliases={} if out is None else {len(pieces): 0},
        cost_estimate=pl.CostEstimate(flops=0, bytes_accessed=8 * 2**20, transcendentals=0),
        compiler_params=params(1),
        name="place_own" if mine else "place_other",
    )(*pieces, *extra)


def gather_output(copies):
    both = ("rows", "tok")
    line = [[chip_id(y, x, z) for z in range(NZ)] for y in range(NY) for x in range(NX)]
    halves = lay_line(lax.all_to_all(copies, "rows", 0, 0, axis_index_groups=line))

    def exchange(value, part, round_one):
        return [
            lax.ppermute(value, both, plane_pairs(o, (part == 0) == round_one)) for o in (1, 2, 3)
        ]

    blocks = [jnp.stack([h] + exchange(h, p, True)) for p, h in enumerate(halves)]
    mine = [piece for p, b in enumerate(blocks) for piece in [b] + exchange(b, p, False)]
    other = [lax.ppermute(piece, "tok", SWAP) for piece in mine]
    return place(False, other, place(True, mine))


def per_device(calib, w_panels, w_trail, keep_mask, factor_block, factor_trail):
    span = factor_block.shape[0]
    local = factor_trail.shape[1]
    chip = lax.axis_index("rows")

    panels_other = lax.ppermute(w_panels, "tok", SWAP)
    keep_other = lax.ppermute(keep_mask, "tok", SWAP)
    cols = lax.dynamic_slice_in_dim(calib, span + chip * local, local, 1)
    projected = lax.dot_general(cols, factor_trail, CONTRACT_LAST, preferred_element_type=F32)
    tie = lax.optimization_barrier
    projected, panels_other, keep_other, w_sent = tie(
        (projected, panels_other, keep_other, w_trail)
    )
    w_other = lax.ppermute(w_sent, "tok", SWAP)
    bases = []
    for step, (axis, bit) in enumerate(REDUCE_STEPS):
        received = lax.ppermute(projected, "rows", gray_pairs(axis, bit))
        if step == 0:
            prepared = prepare(w_panels, panels_other, keep_mask, keep_other, factor_block)
            projected, *prepared = tie((projected + received, *prepared))
        elif step == 1:
            *state, x_all = sweep_first(prepared, calib)
            projected, x_all, *state = tie((projected + received, x_all, *state))
        elif step == 2:
            *swept, pruned, own_all = sweep_second(prepared, state, w_trail)
            projected, w_other, own_all, *swept = tie(
                (projected + received, w_other, own_all, *swept)
            )
        elif step <= 4:
            base = base_product(step - 3, x_all, own_all, w_other)
            projected, base = tie((projected + received, base))
            bases.append(base)
        else:
            projected = projected + received
    return pruned, gather_output(correct(bases, x_all, projected, swept))


def solution(mesh):
    both = P(("rows", "tok"), None)
    return jax.shard_map(
        per_device,
        mesh=mesh,
        in_specs=(P("tok", None), both, both, both, P(), P(None, "rows")),
        out_specs=(both, P()),
        check_vma=False,
    )
```

```python
import functools

import jax
import jax.numpy as jnp
from jax import lax
from jax.experimental import pallas as pl
from jax.experimental.pallas import tpu as pltpu
from jax.sharding import PartitionSpec as P


NY, NX, NZ = 4, 4, 8
CHIPS = NY * NX * NZ
BLOCK = 16
F32 = jnp.float32
BF16 = jnp.bfloat16
VMEM = pl.BlockSpec(memory_space=pltpu.VMEM)
ANY = pl.BlockSpec(memory_space=pl.ANY)
HBM = pl.BlockSpec(memory_space=pltpu.MemorySpace.HBM)
CONTRACT_LAST = (((1,), (1,)), ((), ()))


def chip_id(y, x, z):
    return (y * NX + x) * NZ + z


def coords():
    return [(y, x, z) for y in range(NY) for x in range(NX) for z in range(NZ)]


def gray(i):
    return i ^ (i >> 1)


def gray_pairs(axis, bit):
    position = {gray(i): i for i in range(NZ)}
    pairs = []
    for here in coords():
        there = list(here)
        there[axis] = position[gray(here[axis]) ^ bit]
        pairs.append((chip_id(*here), chip_id(*there)))
    return pairs


REDUCE_STEPS = ((2, 1), (2, 2), (2, 4), (1, 1), (1, 2), (0, 1), (0, 2))


def plane_pairs(offset, first):
    pairs = []
    for y, x, z in coords():
        for t in range(2):
            along_x = (t == 0) == first
            peer = chip_id(y, x ^ offset, z) if along_x else chip_id(y ^ offset, x, z)
            pairs.append((chip_id(y, x, z) * 2 + t, peer * 2 + t))
    return pairs


SWAP = [(0, 1), (1, 0)]


def params(mib):
    return pltpu.CompilerParams(vmem_limit_bytes=mib * 2**20)


def split(v):
    high = v.astype(BF16)
    return high, (v - high.astype(F32)).astype(BF16)


def in_hbm(array):
    return pltpu.with_memory_space_constraint(array, pltpu.MemorySpace.HBM)


def dot(a, b):
    return jnp.dot(a, b, preferred_element_type=F32)


def prepare_kernel(w_own, w_other, keep_own, keep_other, factor_ref,
                   tiles, wt, scale, keep_t, fh, fl, w_all, keep_all, factor_all, sems):
    n = factor_ref.shape[0]
    own = pl.multiple_of(lax.axis_index("tok") * 64, 64)
    other = pl.multiple_of(64 - own, 64)
    loads = [
        pltpu.make_async_copy(factor_ref, factor_all, sems.at[0]),
        pltpu.make_async_copy(w_own, w_all.at[pl.ds(own, 64), :], sems.at[1]),
        pltpu.make_async_copy(keep_own, keep_all.at[pl.ds(own, 64), :], sems.at[2]),
    ]
    for load in loads:
        load.start()
    w_all[pl.ds(other, 64), :] = w_other[...]
    keep_all[pl.ds(other, 64), :] = keep_other[...]
    for load in loads:
        load.wait()
    factor = factor_all[...]
    for block in range(n // BLOCK):
        rows, lanes = block * BLOCK, block * BLOCK // 128 * 128
        tiles[block] = factor_all[rows : rows + BLOCK, lanes : lanes + 128]
    eye = (lax.broadcasted_iota(jnp.int32, (n, n), 0) == lax.broadcasted_iota(jnp.int32, (n, n), 1))
    diag = jnp.sum(jnp.where(eye, factor, 0.0), axis=1, keepdims=True)
    ft_high, ft_low = split(factor.T)
    fh[...] = ft_high
    fl[...] = ft_low
    wt[...] = w_all[...].astype(F32).T
    kept = keep_all[...].astype(F32).T
    keep_t[...] = kept
    scale[...] = (1.0 - kept) * (1.0 / diag)


def prepare(w_own, w_other, keep_own, keep_other, factor):
    n = factor.shape[0]
    tall = jax.ShapeDtypeStruct((n, 128), F32)
    square = jax.ShapeDtypeStruct((n, n), BF16)
    tiles = jax.ShapeDtypeStruct((n // BLOCK, BLOCK, 128), F32)
    return pl.pallas_call(
        prepare_kernel,
        out_shape=(tiles, tall, tall, tall, square, square),
        in_specs=[HBM, VMEM, HBM, VMEM, HBM],
        out_specs=(VMEM,) * 6,
        scratch_shapes=[
            pltpu.VMEM((128, n), BF16),
            pltpu.VMEM((128, n), jnp.int32),
            pltpu.VMEM((n, n), F32),
            pltpu.SemaphoreType.DMA((3,)),
        ],
        cost_estimate=pl.CostEstimate(flops=10**8, bytes_accessed=6 * 2**20, transcendentals=0),
        compiler_params=params(4),
        name="prepare",
    )(in_hbm(w_own), w_other, in_hbm(keep_own), keep_other, in_hbm(factor))


def sweep_blocks(first, count, tiles_ref, wt, scale, keep_t, fh, fl, eh, el, final_t, cur, tiles,
                 tile_sem):
    sub = lax.broadcasted_iota(jnp.int32, (BLOCK, 128), 0)

    def tile_copy(block):
        return pltpu.make_async_copy(
            tiles_ref.at[block], tiles.at[block - first], tile_sem.at[block - first]
        )

    for block in range(first, first + count):
        tile_copy(block).start()

    def advance(block, carry):
        start = pl.multiple_of(block * BLOCK, BLOCK)
        lane = lax.rem(start, 128)
        rows = pl.ds(start, BLOCK)
        tile_copy(block).wait()
        high, low = fh[rows, :], fl[rows, :]
        errs_high = eh[...]
        update = dot(high, errs_high) + dot(low, errs_high) + dot(high, el[...])
        cur[...] = wt[rows, :] - update
        cols = [cur[pl.ds(j, 8, stride=0), :] for j in range(BLOCK)]
        errs = jnp.zeros((BLOCK, 128), F32)
        vals = jnp.zeros((BLOCK, 128), F32)
        for j in range(BLOCK):
            e = cols[j] * scale[pl.ds(start + j, 8, stride=0), :]
            for k in range(j + 1, BLOCK):
                cols[k] = cols[k] - e * tiles[block - first, j, lane + k]
            wide_e = jnp.concatenate([e] * (BLOCK // 8), axis=0)
            wide_c = jnp.concatenate([cols[j]] * (BLOCK // 8), axis=0)
            errs = jnp.where(sub == j, wide_e, errs)
            vals = jnp.where(sub == j, wide_c, vals)
        final_t[rows, :] = vals * keep_t[rows, :]
        e_high, e_low = split(errs)
        eh[rows, :] = e_high
        el[rows, :] = e_low
        return carry

    lax.fori_loop(first, first + count, advance, 0)


def sweep_first_kernel(tiles_ref, wt, scale, keep_t, fh, fl, calib_ref, eh, el, final_t, x_out,
                       cur, tiles, sem, load_sem):
    load = pltpu.make_async_copy(calib_ref, x_out, load_sem)
    load.start()
    eh[...] = jnp.zeros_like(eh)
    el[...] = jnp.zeros_like(el)
    final_t[...] = jnp.zeros_like(final_t)
    count = tiles_ref.shape[0] // 2
    sweep_blocks(0, count, tiles_ref, wt, scale, keep_t, fh, fl, eh, el, final_t, cur, tiles, sem)
    load.wait()


def sweep_second_kernel(tiles_ref, wt, scale, keep_t, fh, fl, eh_in, el_in, final_in, trail_ref,
                        eh, el, fin_high, fin_low, pruned_ref, trail_out,
                        final_t, back, cur, tiles, sem, load_sem):
    load = pltpu.make_async_copy(trail_ref, trail_out, load_sem)
    load.start()
    own = pl.multiple_of(lax.axis_index("tok") * 64, 64)
    eh[...] = eh_in[...]
    el[...] = el_in[...]
    final_t[...] = final_in[...]
    count = tiles_ref.shape[0] // 2
    sweep_blocks(count, count, tiles_ref, wt, scale, keep_t, fh, fl, eh, el, final_t, cur, tiles,
                 sem)
    final = final_t[...]
    high, low = split(final)
    fin_high[...] = high
    fin_low[...] = low
    back[...] = final.T
    pruned_ref[...] = back[pl.ds(own, 64), :].astype(BF16)
    load.wait()


def sweep_scratch(n):
    half = n // BLOCK // 2
    return [
        pltpu.VMEM((BLOCK, 128), F32),
        pltpu.SMEM((half, BLOCK, 128), F32),
        pltpu.SemaphoreType.DMA((half,)),
        pltpu.SemaphoreType.DMA,
    ]


def sweep_first(prepared, calib):
    n = prepared[0].shape[0] * BLOCK
    narrow = jax.ShapeDtypeStruct((n, 128), BF16)
    return pl.pallas_call(
        sweep_first_kernel,
        out_shape=(
            narrow, narrow, jax.ShapeDtypeStruct((n, 128), F32),
            jax.ShapeDtypeStruct(calib.shape, BF16),
        ),
        in_specs=[VMEM] * 6 + [HBM],
        out_specs=(VMEM,) * 4,
        scratch_shapes=sweep_scratch(n),
        cost_estimate=pl.CostEstimate(flops=10**8, bytes_accessed=8 * 2**20, transcendentals=0),
        compiler_params=params(10),
        name="sweep_first",
    )(*prepared, in_hbm(calib))


def sweep_second(prepared, state, w_trail):
    n = prepared[0].shape[0] * BLOCK
    narrow = jax.ShapeDtypeStruct((n, 128), BF16)
    return pl.pallas_call(
        sweep_second_kernel,
        out_shape=(narrow,) * 4
        + (jax.ShapeDtypeStruct((64, n), BF16), jax.ShapeDtypeStruct(w_trail.shape, BF16)),
        in_specs=[VMEM] * 9 + [HBM],
        out_specs=(VMEM,) * 6,
        scratch_shapes=[pltpu.VMEM((n, 128), F32), pltpu.VMEM((128, n), F32)] + sweep_scratch(n),
        cost_estimate=pl.CostEstimate(flops=10**8, bytes_accessed=8 * 2**20, transcendentals=0),
        compiler_params=params(10),
        name="sweep_second",
    )(*prepared, *state, in_hbm(w_trail))


def base_kernel(begin, width, x_ref, own_ref, other_ref, out_ref):
    skip = x_ref.shape[1] - own_ref.shape[1]
    mine = jnp.zeros((64, 64), F32)
    theirs = jnp.zeros((64, 64), F32)
    for at in range(begin, begin + width, CHUNK):
        x = x_ref[:, skip + at : skip + at + CHUNK]
        cols = slice(at, at + CHUNK)
        mine = mine + lax.dot_general(
            x, own_ref[:, cols], CONTRACT_LAST, preferred_element_type=F32
        )
        theirs = theirs + lax.dot_general(
            x, other_ref[:, cols], CONTRACT_LAST, preferred_element_type=F32
        )
    out_ref[0] = mine
    out_ref[1] = theirs


CHUNK = 9 * 128


def base_product(part, x, own, other):
    chunks = own.shape[1] // CHUNK
    begin, end = part * chunks // 2, (part + 1) * chunks // 2
    return pl.pallas_call(
        functools.partial(base_kernel, begin * CHUNK, (end - begin) * CHUNK),
        out_shape=jax.ShapeDtypeStruct((2, 64, 64), F32),
        in_specs=[VMEM] * 3,
        out_specs=VMEM,
        cost_estimate=pl.CostEstimate(flops=10**8, bytes_accessed=8 * 2**20, transcendentals=0),
        compiler_params=params(4),
        name=f"base_product_{part}",
    )(x, own, other)


def correct_kernel(base_0, base_1, x_ref, proj_ref, eh_ref, el_ref, fh_ref, fl_ref,
                   out_ref):
    p_high, p_low = split(proj_ref[...])
    e_high, e_low = eh_ref[...], el_ref[...]
    x = x_ref[:, : eh_ref.shape[0]]
    mine = base_0[0] + base_1[0]
    theirs = base_0[1] + base_1[1]
    first = lax.axis_index("tok") == 0
    base = jnp.concatenate(
        [jnp.where(first, mine, theirs), jnp.where(first, theirs, mine)], axis=1
    )
    base = base + (dot(x, fh_ref[...]) + dot(x, fl_ref[...]))
    fix = dot(p_high, e_high) + dot(p_high, e_low) + dot(p_low, e_high)
    out = (base - fix).astype(BF16)
    out_ref[...] = jnp.broadcast_to(out[None], out_ref.shape)


def correct(bases, x_all, projected, swept):
    return pl.pallas_call(
        correct_kernel,
        out_shape=jax.ShapeDtypeStruct((NZ, 64, 128), BF16),
        in_specs=[VMEM] * 8,
        out_specs=VMEM,
        cost_estimate=pl.CostEstimate(flops=10**7, bytes_accessed=2**20, transcendentals=0),
        compiler_params=params(4),
        name="correct",
    )(*bases, x_all, projected, *swept)


def lay_line_kernel(in_ref, low_ref, high_ref):
    for z in range(NZ):
        low_ref[:, z * 128 : (z + 1) * 128] = in_ref[z, :32, :]
        high_ref[:, z * 128 : (z + 1) * 128] = in_ref[z, 32:, :]


def lay_line(gathered):
    half = jax.ShapeDtypeStruct((32, NZ * 128), BF16)
    return pl.pallas_call(
        lay_line_kernel,
        out_shape=(half, half),
        in_specs=[VMEM],
        out_specs=(VMEM, VMEM),
        compiler_params=params(2),
        name="lay_line",
    )(gathered)


def place_kernel(mine, *refs):
    pieces, out_ref, sem = refs[:8], refs[-2], refs[-1]
    chip = lax.axis_index("rows")
    t = lax.axis_index("tok")
    y, x = chip // (NX * NZ), lax.rem(chip // NZ, NX)
    core = t if mine else 1 - t
    copies = []
    for part in range(2):
        x_first = core == part
        rows = pl.ds(pl.multiple_of(core * 64 + part * 32, 32), 32)
        for second in range(4):
            for first in range(4):
                x_at = jnp.where(x_first, x ^ first, x ^ second)
                y_at = jnp.where(x_first, y ^ second, y ^ first)
                cols = pl.ds(pl.multiple_of((y_at * NX + x_at) * (NZ * 128), NZ * 128), NZ * 128)
                copies.append(
                    pltpu.make_async_copy(
                        pieces[part * 4 + second].at[first], out_ref.at[rows, cols],
                        sem.at[len(copies)],
                    )
                )
                copies[-1].start()
    for copy in copies:
        copy.wait()


def place(mine, pieces, out=None):
    extra = () if out is None else (out,)
    return pl.pallas_call(
        functools.partial(place_kernel, mine),
        out_shape=jax.ShapeDtypeStruct((128, CHIPS * 128), BF16),
        in_specs=[ANY] * (len(pieces) + len(extra)),
        out_specs=ANY,
        scratch_shapes=[pltpu.SemaphoreType.DMA((32,))],
        input_output_aliases={} if out is None else {len(pieces): 0},
        cost_estimate=pl.CostEstimate(flops=0, bytes_accessed=8 * 2**20, transcendentals=0),
        compiler_params=params(1),
        name="place_own" if mine else "place_other",
    )(*pieces, *extra)


def gather_output(copies):
    both = ("rows", "tok")
    line = [[chip_id(y, x, z) for z in range(NZ)] for y in range(NY) for x in range(NX)]
    halves = lay_line(lax.all_to_all(copies, "rows", 0, 0, axis_index_groups=line))

    def exchange(value, part, round_one):
        return [
            lax.ppermute(value, both, plane_pairs(o, (part == 0) == round_one)) for o in (1, 2, 3)
        ]

    blocks = [jnp.stack([h] + exchange(h, p, True)) for p, h in enumerate(halves)]
    mine = [piece for p, b in enumerate(blocks) for piece in [b] + exchange(b, p, False)]
    other = [lax.ppermute(piece, "tok", SWAP) for piece in mine]
    return place(False, other, place(True, mine))


def per_device(calib, w_panels, w_trail, keep_mask, factor_block, factor_trail):
    span = factor_block.shape[0]
    local = factor_trail.shape[1]
    chip = lax.axis_index("rows")

    panels_other = lax.ppermute(w_panels, "tok", SWAP)
    keep_other = lax.ppermute(keep_mask, "tok", SWAP)
    cols = lax.dynamic_slice_in_dim(calib, span + chip * local, local, 1)
    projected = lax.dot_general(cols, factor_trail, CONTRACT_LAST, preferred_element_type=F32)
    tie = lax.optimization_barrier
    projected, panels_other, keep_other, w_sent = tie(
        (projected, panels_other, keep_other, w_trail)
    )
    w_other = lax.ppermute(w_sent, "tok", SWAP)
    bases = []
    for step, (axis, bit) in enumerate(REDUCE_STEPS):
        received = lax.ppermute(projected, "rows", gray_pairs(axis, bit))
        if step == 0:
            prepared = prepare(w_panels, panels_other, keep_mask, keep_other, factor_block)
            projected, *prepared = tie((projected + received, *prepared))
        elif step == 1:
            *state, x_all = sweep_first(prepared, calib)
            projected, x_all, *state = tie((projected + received, x_all, *state))
        elif step == 2:
            *swept, pruned, own_all = sweep_second(prepared, state, w_trail)
            projected, w_other, own_all, *swept = tie(
                (projected + received, w_other, own_all, *swept)
            )
        elif step <= 4:
            base = base_product(step - 3, x_all, own_all, w_other)
            projected, base = tie((projected + received, base))
            bases.append(base)
        else:
            projected = projected + received
    return pruned, gather_output(correct(bases, x_all, projected, swept))


def solution(mesh):
    both = P(("rows", "tok"), None)
    return jax.shard_map(
        per_device,
        mesh=mesh,
        in_specs=(P("tok", None), both, both, both, P(), P(None, "rows")),
        out_specs=(both, P()),
        check_vma=False,
    )
```

```python
import functools

import jax
import jax.numpy as jnp
from jax import lax
from jax.experimental import pallas as pl
from jax.experimental.pallas import tpu as pltpu
from jax.sharding import PartitionSpec as P


NY, NX, NZ = 4, 4, 8
CHIPS = NY * NX * NZ
BLOCK = 16
PARTS = (5, 5)
F32 = jnp.float32
BF16 = jnp.bfloat16
VMEM = pl.BlockSpec(memory_space=pltpu.VMEM)
ANY = pl.BlockSpec(memory_space=pl.ANY)
HBM = pl.BlockSpec(memory_space=pltpu.MemorySpace.HBM)
CONTRACT_LAST = (((1,), (1,)), ((), ()))


def chip_id(y, x, z):
    return (y * NX + x) * NZ + z


def coords():
    return [(y, x, z) for y in range(NY) for x in range(NX) for z in range(NZ)]


def gray(i):
    return i ^ (i >> 1)


def gray_pairs(axis, bit):
    position = {gray(i): i for i in range(NZ)}
    pairs = []
    for here in coords():
        there = list(here)
        there[axis] = position[gray(here[axis]) ^ bit]
        pairs.append((chip_id(*here), chip_id(*there)))
    return pairs


REDUCE_STEPS = ((2, 1), (2, 2), (2, 4), (1, 1), (1, 2), (0, 1), (0, 2))


def plane_pairs(offset, first):
    pairs = []
    for y, x, z in coords():
        for t in range(2):
            peer = chip_id(y, x ^ offset, z) if first else chip_id(y ^ offset, x, z)
            pairs.append((chip_id(y, x, z) * 2 + t, peer * 2 + t))
    return pairs


SWAP = [(0, 1), (1, 0)]


def params(mib):
    return pltpu.CompilerParams(vmem_limit_bytes=mib * 2**20)


def split(v):
    high = v.astype(BF16)
    return high, (v - high.astype(F32)).astype(BF16)


def in_hbm(array):
    return pltpu.with_memory_space_constraint(array, pltpu.MemorySpace.HBM)


def dot(a, b):
    return jnp.dot(a, b, preferred_element_type=F32)


def prepare_kernel(w_own, w_other, keep_own, keep_other, factor_ref,
                   tiles, wt, scale, keep_t, fh, fl, w_all, keep_all, factor_all, sems):
    n = factor_ref.shape[0]
    own = pl.multiple_of(lax.axis_index("tok") * 64, 64)
    other = pl.multiple_of(64 - own, 64)
    loads = [
        pltpu.make_async_copy(factor_ref, factor_all, sems.at[0]),
        pltpu.make_async_copy(w_own, w_all.at[pl.ds(own, 64), :], sems.at[1]),
        pltpu.make_async_copy(keep_own, keep_all.at[pl.ds(own, 64), :], sems.at[2]),
    ]
    for load in loads:
        load.start()
    w_all[pl.ds(other, 64), :] = w_other[...]
    keep_all[pl.ds(other, 64), :] = keep_other[...]
    for load in loads:
        load.wait()
    factor = factor_all[...]
    for block in range(n // BLOCK):
        rows, lanes = block * BLOCK, block * BLOCK // 128 * 128
        tiles[block] = factor_all[rows : rows + BLOCK, lanes : lanes + 128]
    eye = (lax.broadcasted_iota(jnp.int32, (n, n), 0) == lax.broadcasted_iota(jnp.int32, (n, n), 1))
    diag = jnp.sum(jnp.where(eye, factor, 0.0), axis=1, keepdims=True)
    ft_high, ft_low = split(factor.T)
    fh[...] = ft_high
    fl[...] = ft_low
    wt[...] = w_all[...].astype(F32).T
    kept = keep_all[...].astype(F32).T
    keep_t[...] = kept
    scale[...] = (1.0 - kept) * (1.0 / diag)


def prepare(w_own, w_other, keep_own, keep_other, factor):
    n = factor.shape[0]
    tall = jax.ShapeDtypeStruct((n, 128), F32)
    square = jax.ShapeDtypeStruct((n, n), BF16)
    tiles = jax.ShapeDtypeStruct((n // BLOCK, BLOCK, 128), F32)
    return pl.pallas_call(
        prepare_kernel,
        out_shape=(tiles, tall, tall, tall, square, square),
        in_specs=[HBM, VMEM, HBM, VMEM, HBM],
        out_specs=(VMEM,) * 6,
        scratch_shapes=[
            pltpu.VMEM((128, n), BF16),
            pltpu.VMEM((128, n), jnp.int32),
            pltpu.VMEM((n, n), F32),
            pltpu.SemaphoreType.DMA((3,)),
        ],
        cost_estimate=pl.CostEstimate(flops=10**8, bytes_accessed=6 * 2**20, transcendentals=0),
        compiler_params=params(4),
        name="prepare",
    )(in_hbm(w_own), w_other, in_hbm(keep_own), keep_other, in_hbm(factor))


def sweep_blocks(first, count, tiles_ref, wt, scale, keep_t, fh, fl, eh, el, final_t, cur, tiles,
                 tile_sem):
    sub = lax.broadcasted_iota(jnp.int32, (BLOCK, 128), 0)

    def tile_copy(block):
        return pltpu.make_async_copy(
            tiles_ref.at[block], tiles.at[block - first], tile_sem.at[block - first]
        )

    for block in range(first, first + count):
        tile_copy(block).start()

    def advance(block, carry):
        start = pl.multiple_of(block * BLOCK, BLOCK)
        lane = lax.rem(start, 128)
        rows = pl.ds(start, BLOCK)
        tile_copy(block).wait()
        high, low = fh[rows, :], fl[rows, :]
        errs_high = eh[...]
        update = dot(high, errs_high) + dot(low, errs_high) + dot(high, el[...])
        cur[...] = wt[rows, :] - update
        cols = [cur[pl.ds(j, 8, stride=0), :] for j in range(BLOCK)]
        errs = jnp.zeros((BLOCK, 128), F32)
        vals = jnp.zeros((BLOCK, 128), F32)
        for j in range(BLOCK):
            e = cols[j] * scale[pl.ds(start + j, 8, stride=0), :]
            for k in range(j + 1, BLOCK):
                cols[k] = cols[k] - e * tiles[block - first, j, lane + k]
            wide_e = jnp.concatenate([e] * (BLOCK // 8), axis=0)
            wide_c = jnp.concatenate([cols[j]] * (BLOCK // 8), axis=0)
            errs = jnp.where(sub == j, wide_e, errs)
            vals = jnp.where(sub == j, wide_c, vals)
        final_t[rows, :] = vals * keep_t[rows, :]
        e_high, e_low = split(errs)
        eh[rows, :] = e_high
        el[rows, :] = e_low
        return carry

    lax.fori_loop(first, first + count, advance, 0)


def sweep_first_kernel(tiles_ref, wt, scale, keep_t, fh, fl, calib_ref, eh, el, final_t, x_out,
                       cur, tiles, sem, load_sem):
    load = pltpu.make_async_copy(calib_ref, x_out, load_sem)
    load.start()
    eh[...] = jnp.zeros_like(eh)
    el[...] = jnp.zeros_like(el)
    final_t[...] = jnp.zeros_like(final_t)
    sweep_blocks(0, PARTS[0], tiles_ref, wt, scale, keep_t, fh, fl, eh, el, final_t, cur, tiles, sem)
    load.wait()


def sweep_middle_kernel(tiles_ref, wt, scale, keep_t, fh, fl, eh_in, el_in, final_in,
                        eh, el, final_t, cur, tiles, sem):
    eh[...] = eh_in[...]
    el[...] = el_in[...]
    final_t[...] = final_in[...]
    sweep_blocks(PARTS[0], PARTS[1], tiles_ref, wt, scale, keep_t, fh, fl, eh, el, final_t, cur,
                 tiles, sem)


def sweep_last_kernel(tiles_ref, wt, scale, keep_t, fh, fl, eh_in, el_in, final_in, trail_ref,
                      eh, el, fin_high, fin_low, pruned_ref, trail_out,
                      final_t, back, cur, tiles, sem, load_sem):
    load = pltpu.make_async_copy(trail_ref, trail_out, load_sem)
    load.start()
    own = pl.multiple_of(lax.axis_index("tok") * 64, 64)
    eh[...] = eh_in[...]
    el[...] = el_in[...]
    final_t[...] = final_in[...]
    done = PARTS[0] + PARTS[1]
    sweep_blocks(done, tiles_ref.shape[0] - done, tiles_ref, wt, scale, keep_t, fh, fl, eh, el,
                 final_t, cur, tiles, sem)
    final = final_t[...]
    high, low = split(final)
    fin_high[...] = high
    fin_low[...] = low
    back[...] = final.T
    pruned_ref[...] = back[pl.ds(own, 64), :].astype(BF16)
    load.wait()


def sweep_scratch(count):
    return [
        pltpu.VMEM((BLOCK, 128), F32),
        pltpu.SMEM((count, BLOCK, 128), F32),
        pltpu.SemaphoreType.DMA((count,)),
    ]


SWEEP_COST = pl.CostEstimate(flops=10**8, bytes_accessed=8 * 2**20, transcendentals=0)


def sweep_first(prepared, calib):
    n = prepared[0].shape[0] * BLOCK
    narrow = jax.ShapeDtypeStruct((n, 128), BF16)
    return pl.pallas_call(
        sweep_first_kernel,
        out_shape=(
            narrow, narrow, jax.ShapeDtypeStruct((n, 128), F32),
            jax.ShapeDtypeStruct(calib.shape, BF16),
        ),
        in_specs=[VMEM] * 6 + [HBM],
        out_specs=(VMEM,) * 4,
        scratch_shapes=sweep_scratch(PARTS[0]) + [pltpu.SemaphoreType.DMA],
        cost_estimate=SWEEP_COST,
        compiler_params=params(10),
        name="sweep_first",
    )(*prepared, in_hbm(calib))


def sweep_middle(prepared, state):
    n = prepared[0].shape[0] * BLOCK
    narrow = jax.ShapeDtypeStruct((n, 128), BF16)
    return pl.pallas_call(
        sweep_middle_kernel,
        out_shape=(narrow, narrow, jax.ShapeDtypeStruct((n, 128), F32)),
        in_specs=[VMEM] * 9,
        out_specs=(VMEM,) * 3,
        scratch_shapes=sweep_scratch(PARTS[1]),
        cost_estimate=SWEEP_COST,
        compiler_params=params(6),
        name="sweep_middle",
    )(*prepared, *state)


def sweep_last(prepared, state, w_trail):
    n = prepared[0].shape[0] * BLOCK
    narrow = jax.ShapeDtypeStruct((n, 128), BF16)
    count = prepared[0].shape[0] - PARTS[0] - PARTS[1]
    return pl.pallas_call(
        sweep_last_kernel,
        out_shape=(narrow,) * 4
        + (jax.ShapeDtypeStruct((64, n), BF16), jax.ShapeDtypeStruct(w_trail.shape, BF16)),
        in_specs=[VMEM] * 9 + [HBM],
        out_specs=(VMEM,) * 6,
        scratch_shapes=[pltpu.VMEM((n, 128), F32), pltpu.VMEM((128, n), F32)]
        + sweep_scratch(count)
        + [pltpu.SemaphoreType.DMA],
        cost_estimate=SWEEP_COST,
        compiler_params=params(10),
        name="sweep_last",
    )(*prepared, *state, in_hbm(w_trail))


def base_kernel(begin, width, x_ref, own_ref, other_ref, out_ref):
    skip = x_ref.shape[1] - own_ref.shape[1]
    mine = jnp.zeros((64, 64), F32)
    theirs = jnp.zeros((64, 64), F32)
    for at in range(begin, begin + width, CHUNK):
        x = x_ref[:, skip + at : skip + at + CHUNK]
        cols = slice(at, at + CHUNK)
        mine = mine + lax.dot_general(
            x, own_ref[:, cols], CONTRACT_LAST, preferred_element_type=F32
        )
        theirs = theirs + lax.dot_general(
            x, other_ref[:, cols], CONTRACT_LAST, preferred_element_type=F32
        )
    out_ref[0] = mine
    out_ref[1] = theirs


CHUNK = 9 * 128


def base_product(part, x, own, other):
    chunks = own.shape[1] // CHUNK
    begin, end = part * chunks // 2, (part + 1) * chunks // 2
    return pl.pallas_call(
        functools.partial(base_kernel, begin * CHUNK, (end - begin) * CHUNK),
        out_shape=jax.ShapeDtypeStruct((2, 64, 64), F32),
        in_specs=[VMEM] * 3,
        out_specs=VMEM,
        cost_estimate=pl.CostEstimate(flops=10**8, bytes_accessed=8 * 2**20, transcendentals=0),
        compiler_params=params(4),
        name=f"base_product_{part}",
    )(x, own, other)


def correct_kernel(base_0, base_1, x_ref, proj_ref, eh_ref, el_ref, fh_ref, fl_ref,
                   out_ref):
    p_high, p_low = split(proj_ref[...])
    e_high, e_low = eh_ref[...], el_ref[...]
    x = x_ref[:, : eh_ref.shape[0]]
    mine = base_0[0] + base_1[0]
    theirs = base_0[1] + base_1[1]
    first = lax.axis_index("tok") == 0
    base = jnp.concatenate(
        [jnp.where(first, mine, theirs), jnp.where(first, theirs, mine)], axis=1
    )
    base = base + (dot(x, fh_ref[...]) + dot(x, fl_ref[...]))
    fix = dot(p_high, e_high) + dot(p_high, e_low) + dot(p_low, e_high)
    out = (base - fix).astype(BF16)
    out_ref[...] = jnp.broadcast_to(out[None], out_ref.shape)


def correct(bases, x_all, projected, swept):
    return pl.pallas_call(
        correct_kernel,
        out_shape=jax.ShapeDtypeStruct((NZ, 64, 128), BF16),
        in_specs=[VMEM] * 8,
        out_specs=VMEM,
        cost_estimate=pl.CostEstimate(flops=10**7, bytes_accessed=2**20, transcendentals=0),
        compiler_params=params(4),
        name="correct",
    )(*bases, x_all, projected, *swept)


def lay_line_kernel(in_ref, low_ref, high_ref):
    for z in range(NZ):
        low_ref[:, z * 128 : (z + 1) * 128] = in_ref[z, :32, :]
        high_ref[:, z * 128 : (z + 1) * 128] = in_ref[z, 32:, :]


def lay_line(gathered):
    half = jax.ShapeDtypeStruct((32, NZ * 128), BF16)
    return pl.pallas_call(
        lay_line_kernel,
        out_shape=(half, half),
        in_specs=[VMEM],
        out_specs=(VMEM, VMEM),
        compiler_params=params(2),
        name="lay_line",
    )(gathered)


def place_kernel(mine, *refs):
    pieces, out_ref, sem = refs[:8], refs[-2], refs[-1]
    chip = lax.axis_index("rows")
    t = lax.axis_index("tok")
    y, x = chip // (NX * NZ), lax.rem(chip // NZ, NX)
    core = t if mine else 1 - t
    copies = []
    for part in range(2):
        x_first = part == 0
        rows = pl.ds(pl.multiple_of(core * 64 + part * 32, 32), 32)
        for second in range(4):
            for first in range(4):
                x_at = x ^ (first if x_first else second)
                y_at = y ^ (second if x_first else first)
                cols = pl.ds(pl.multiple_of((y_at * NX + x_at) * (NZ * 128), NZ * 128), NZ * 128)
                copies.append(
                    pltpu.make_async_copy(
                        pieces[part * 4 + second].at[first], out_ref.at[rows, cols],
                        sem.at[len(copies)],
                    )
                )
                copies[-1].start()
    for copy in copies:
        copy.wait()


def place(mine, pieces, out=None):
    extra = () if out is None else (out,)
    return pl.pallas_call(
        functools.partial(place_kernel, mine),
        out_shape=jax.ShapeDtypeStruct((128, CHIPS * 128), BF16),
        in_specs=[ANY] * (len(pieces) + len(extra)),
        out_specs=ANY,
        scratch_shapes=[pltpu.SemaphoreType.DMA((32,))],
        input_output_aliases={} if out is None else {len(pieces): 0},
        cost_estimate=pl.CostEstimate(flops=0, bytes_accessed=8 * 2**20, transcendentals=0),
        compiler_params=params(1),
        name="place_own" if mine else "place_other",
    )(*pieces, *extra)


def gather_output(copies):
    both = ("rows", "tok")
    line = [[chip_id(y, x, z) for z in range(NZ)] for y in range(NY) for x in range(NX)]
    halves = lay_line(lax.all_to_all(copies, "rows", 0, 0, axis_index_groups=line))

    def exchange(value, part, round_one):
        return [
            lax.ppermute(value, both, plane_pairs(o, (part == 0) == round_one)) for o in (1, 2, 3)
        ]

    blocks = [jnp.stack([h] + exchange(h, p, True)) for p, h in enumerate(halves)]
    mine = [piece for p, b in enumerate(blocks) for piece in [b] + exchange(b, p, False)]
    other = [lax.ppermute(piece, "tok", SWAP) for piece in mine]
    return place(False, other, place(True, mine))


def per_device(calib, w_panels, w_trail, keep_mask, factor_block, factor_trail):
    span = factor_block.shape[0]
    local = factor_trail.shape[1]
    chip = lax.axis_index("rows")

    panels_other = lax.ppermute(w_panels, "tok", SWAP)
    keep_other = lax.ppermute(keep_mask, "tok", SWAP)
    cols = lax.dynamic_slice_in_dim(calib, span + chip * local, local, 1)
    projected = lax.dot_general(cols, factor_trail, CONTRACT_LAST, preferred_element_type=F32)
    tie = lax.optimization_barrier
    projected, panels_other, keep_other, w_sent = tie(
        (projected, panels_other, keep_other, w_trail)
    )
    w_other = lax.ppermute(w_sent, "tok", SWAP)
    for step, (axis, bit) in enumerate(REDUCE_STEPS):
        received = lax.ppermute(projected, "rows", gray_pairs(axis, bit))
        if step == 0:
            prepared = prepare(w_panels, panels_other, keep_mask, keep_other, factor_block)
            projected, *prepared = tie((projected + received, *prepared))
        elif step == 1:
            *state, x_all = sweep_first(prepared, calib)
            projected, x_all, *state = tie((projected + received, x_all, *state))
        elif step == 2:
            state = sweep_middle(prepared, state)
            projected, *state = tie((projected + received, *state))
        elif step == 3:
            *swept, pruned, own_all = sweep_last(prepared, state, w_trail)
            projected, w_other, own_all, *swept = tie(
                (projected + received, w_other, own_all, *swept)
            )
        elif step == 4:
            bases = [base_product(part, x_all, own_all, w_other) for part in range(2)]
            projected, *bases = tie((projected + received, *bases))
        else:
            projected = projected + received
    return pruned, gather_output(correct(bases, x_all, projected, swept))


def solution(mesh):
    both = P(("rows", "tok"), None)
    return jax.shard_map(
        per_device,
        mesh=mesh,
        in_specs=(P("tok", None), both, both, both, P(), P(None, "rows")),
        out_specs=(both, P()),
        check_vma=False,
    )
```

```python
import functools

import jax
import jax.numpy as jnp
from jax import lax
from jax.experimental import pallas as pl
from jax.experimental.pallas import tpu as pltpu
from jax.sharding import PartitionSpec as P


NY, NX, NZ = 4, 4, 8
CHIPS = NY * NX * NZ
BLOCK = 16
PARTS = (4, 6)
F32 = jnp.float32
BF16 = jnp.bfloat16
VMEM = pl.BlockSpec(memory_space=pltpu.VMEM)
ANY = pl.BlockSpec(memory_space=pl.ANY)
HBM = pl.BlockSpec(memory_space=pltpu.MemorySpace.HBM)
CONTRACT_LAST = (((1,), (1,)), ((), ()))


def chip_id(y, x, z):
    return (y * NX + x) * NZ + z


def coords():
    return [(y, x, z) for y in range(NY) for x in range(NX) for z in range(NZ)]


def gray(i):
    return i ^ (i >> 1)


def gray_pairs(axis, bit):
    position = {gray(i): i for i in range(NZ)}
    pairs = []
    for here in coords():
        there = list(here)
        there[axis] = position[gray(here[axis]) ^ bit]
        pairs.append((chip_id(*here), chip_id(*there)))
    return pairs


REDUCE_STEPS = ((2, 1), (2, 2), (2, 4), (1, 1), (1, 2), (0, 1), (0, 2))


def plane_pairs(offset, first):
    pairs = []
    for y, x, z in coords():
        for t in range(2):
            peer = chip_id(y, x ^ offset, z) if first else chip_id(y ^ offset, x, z)
            pairs.append((chip_id(y, x, z) * 2 + t, peer * 2 + t))
    return pairs


SWAP = [(0, 1), (1, 0)]


def params(mib):
    return pltpu.CompilerParams(vmem_limit_bytes=mib * 2**20)


def split(v):
    high = v.astype(BF16)
    return high, (v - high.astype(F32)).astype(BF16)


def in_hbm(array):
    return pltpu.with_memory_space_constraint(array, pltpu.MemorySpace.HBM)


def dot(a, b):
    return jnp.dot(a, b, preferred_element_type=F32)


def prepare_kernel(w_own, w_other, keep_own, keep_other, factor_ref,
                   tiles, wt, scale, keep_t, fh, fl, w_all, keep_all, factor_all, sems):
    n = factor_ref.shape[0]
    own = pl.multiple_of(lax.axis_index("tok") * 64, 64)
    other = pl.multiple_of(64 - own, 64)
    loads = [
        pltpu.make_async_copy(factor_ref, factor_all, sems.at[0]),
        pltpu.make_async_copy(w_own, w_all.at[pl.ds(own, 64), :], sems.at[1]),
        pltpu.make_async_copy(keep_own, keep_all.at[pl.ds(own, 64), :], sems.at[2]),
    ]
    for load in loads:
        load.start()
    w_all[pl.ds(other, 64), :] = w_other[...]
    keep_all[pl.ds(other, 64), :] = keep_other[...]
    for load in loads:
        load.wait()
    factor = factor_all[...]
    for block in range(n // BLOCK):
        rows, lanes = block * BLOCK, block * BLOCK // 128 * 128
        tiles[block] = factor_all[rows : rows + BLOCK, lanes : lanes + 128]
    eye = (lax.broadcasted_iota(jnp.int32, (n, n), 0) == lax.broadcasted_iota(jnp.int32, (n, n), 1))
    diag = jnp.sum(jnp.where(eye, factor, 0.0), axis=1, keepdims=True)
    ft_high, ft_low = split(factor.T)
    fh[...] = ft_high
    fl[...] = ft_low
    wt[...] = w_all[...].astype(F32).T
    kept = keep_all[...].astype(F32).T
    keep_t[...] = kept
    scale[...] = (1.0 - kept) * (1.0 / diag)


def prepare(w_own, w_other, keep_own, keep_other, factor):
    n = factor.shape[0]
    tall = jax.ShapeDtypeStruct((n, 128), F32)
    square = jax.ShapeDtypeStruct((n, n), BF16)
    tiles = jax.ShapeDtypeStruct((n // BLOCK, BLOCK, 128), F32)
    return pl.pallas_call(
        prepare_kernel,
        out_shape=(tiles, tall, tall, tall, square, square),
        in_specs=[HBM, VMEM, HBM, VMEM, HBM],
        out_specs=(VMEM,) * 6,
        scratch_shapes=[
            pltpu.VMEM((128, n), BF16),
            pltpu.VMEM((128, n), jnp.int32),
            pltpu.VMEM((n, n), F32),
            pltpu.SemaphoreType.DMA((3,)),
        ],
        cost_estimate=pl.CostEstimate(flops=10**8, bytes_accessed=6 * 2**20, transcendentals=0),
        compiler_params=params(4),
        name="prepare",
    )(in_hbm(w_own), w_other, in_hbm(keep_own), keep_other, in_hbm(factor))


def sweep_blocks(first, count, tiles_ref, wt, scale, keep_t, fh, fl, eh, el, final_t, cur, tiles,
                 tile_sem):
    sub = lax.broadcasted_iota(jnp.int32, (BLOCK, 128), 0)

    def tile_copy(block):
        return pltpu.make_async_copy(
            tiles_ref.at[block], tiles.at[block - first], tile_sem.at[block - first]
        )

    for block in range(first, first + count):
        tile_copy(block).start()

    def advance(block, carry):
        start = pl.multiple_of(block * BLOCK, BLOCK)
        lane = lax.rem(start, 128)
        rows = pl.ds(start, BLOCK)
        tile_copy(block).wait()
        high, low = fh[rows, :], fl[rows, :]
        errs_high = eh[...]
        update = dot(high, errs_high) + dot(low, errs_high) + dot(high, el[...])
        cur[...] = wt[rows, :] - update
        cols = [cur[pl.ds(j, 8, stride=0), :] for j in range(BLOCK)]
        errs = jnp.zeros((BLOCK, 128), F32)
        vals = jnp.zeros((BLOCK, 128), F32)
        for j in range(BLOCK):
            e = cols[j] * scale[pl.ds(start + j, 8, stride=0), :]
            for k in range(j + 1, BLOCK):
                cols[k] = cols[k] - e * tiles[block - first, j, lane + k]
            wide_e = jnp.concatenate([e] * (BLOCK // 8), axis=0)
            wide_c = jnp.concatenate([cols[j]] * (BLOCK // 8), axis=0)
            errs = jnp.where(sub == j, wide_e, errs)
            vals = jnp.where(sub == j, wide_c, vals)
        final_t[rows, :] = vals * keep_t[rows, :]
        e_high, e_low = split(errs)
        eh[rows, :] = e_high
        el[rows, :] = e_low
        return carry

    lax.fori_loop(first, first + count, advance, 0)


def sweep_first_kernel(tiles_ref, wt, scale, keep_t, fh, fl, calib_ref, eh, el, final_t, x_out,
                       cur, tiles, sem, load_sem):
    load = pltpu.make_async_copy(calib_ref, x_out, load_sem)
    load.start()
    eh[...] = jnp.zeros_like(eh)
    el[...] = jnp.zeros_like(el)
    final_t[...] = jnp.zeros_like(final_t)
    sweep_blocks(0, PARTS[0], tiles_ref, wt, scale, keep_t, fh, fl, eh, el, final_t, cur, tiles, sem)
    load.wait()


def sweep_middle_kernel(tiles_ref, wt, scale, keep_t, fh, fl, eh_in, el_in, final_in,
                        eh, el, final_t, cur, tiles, sem):
    eh[...] = eh_in[...]
    el[...] = el_in[...]
    final_t[...] = final_in[...]
    sweep_blocks(PARTS[0], PARTS[1], tiles_ref, wt, scale, keep_t, fh, fl, eh, el, final_t, cur,
                 tiles, sem)


def sweep_last_kernel(tiles_ref, wt, scale, keep_t, fh, fl, eh_in, el_in, final_in, trail_ref,
                      eh, el, fin_high, fin_low, pruned_ref, trail_out,
                      final_t, back, cur, tiles, sem, load_sem):
    load = pltpu.make_async_copy(trail_ref, trail_out, load_sem)
    load.start()
    own = pl.multiple_of(lax.axis_index("tok") * 64, 64)
    eh[...] = eh_in[...]
    el[...] = el_in[...]
    final_t[...] = final_in[...]
    done = PARTS[0] + PARTS[1]
    sweep_blocks(done, tiles_ref.shape[0] - done, tiles_ref, wt, scale, keep_t, fh, fl, eh, el,
                 final_t, cur, tiles, sem)
    final = final_t[...]
    high, low = split(final)
    fin_high[...] = high
    fin_low[...] = low
    back[...] = final.T
    pruned_ref[...] = back[pl.ds(own, 64), :].astype(BF16)
    load.wait()


def sweep_scratch(count):
    return [
        pltpu.VMEM((BLOCK, 128), F32),
        pltpu.SMEM((count, BLOCK, 128), F32),
        pltpu.SemaphoreType.DMA((count,)),
    ]


SWEEP_COST = pl.CostEstimate(flops=10**8, bytes_accessed=8 * 2**20, transcendentals=0)


def sweep_first(prepared, calib):
    n = prepared[0].shape[0] * BLOCK
    narrow = jax.ShapeDtypeStruct((n, 128), BF16)
    return pl.pallas_call(
        sweep_first_kernel,
        out_shape=(
            narrow, narrow, jax.ShapeDtypeStruct((n, 128), F32),
            jax.ShapeDtypeStruct(calib.shape, BF16),
        ),
        in_specs=[VMEM] * 6 + [HBM],
        out_specs=(VMEM,) * 4,
        scratch_shapes=sweep_scratch(PARTS[0]) + [pltpu.SemaphoreType.DMA],
        cost_estimate=SWEEP_COST,
        compiler_params=params(10),
        name="sweep_first",
    )(*prepared, in_hbm(calib))


def sweep_middle(prepared, state):
    n = prepared[0].shape[0] * BLOCK
    narrow = jax.ShapeDtypeStruct((n, 128), BF16)
    return pl.pallas_call(
        sweep_middle_kernel,
        out_shape=(narrow, narrow, jax.ShapeDtypeStruct((n, 128), F32)),
        in_specs=[VMEM] * 9,
        out_specs=(VMEM,) * 3,
        scratch_shapes=sweep_scratch(PARTS[1]),
        cost_estimate=SWEEP_COST,
        compiler_params=params(6),
        name="sweep_middle",
    )(*prepared, *state)


def sweep_last(prepared, state, w_trail):
    n = prepared[0].shape[0] * BLOCK
    narrow = jax.ShapeDtypeStruct((n, 128), BF16)
    count = prepared[0].shape[0] - PARTS[0] - PARTS[1]
    return pl.pallas_call(
        sweep_last_kernel,
        out_shape=(narrow,) * 4
        + (jax.ShapeDtypeStruct((64, n), BF16), jax.ShapeDtypeStruct(w_trail.shape, BF16)),
        in_specs=[VMEM] * 9 + [HBM],
        out_specs=(VMEM,) * 6,
        scratch_shapes=[pltpu.VMEM((n, 128), F32), pltpu.VMEM((128, n), F32)]
        + sweep_scratch(count)
        + [pltpu.SemaphoreType.DMA],
        cost_estimate=SWEEP_COST,
        compiler_params=params(10),
        name="sweep_last",
    )(*prepared, *state, in_hbm(w_trail))


def base_kernel(begin, width, x_ref, own_ref, other_ref, out_ref):
    skip = x_ref.shape[1] - own_ref.shape[1]
    mine = jnp.zeros((64, 64), F32)
    theirs = jnp.zeros((64, 64), F32)
    for at in range(begin, begin + width, CHUNK):
        x = x_ref[:, skip + at : skip + at + CHUNK]
        cols = slice(at, at + CHUNK)
        mine = mine + lax.dot_general(
            x, own_ref[:, cols], CONTRACT_LAST, preferred_element_type=F32
        )
        theirs = theirs + lax.dot_general(
            x, other_ref[:, cols], CONTRACT_LAST, preferred_element_type=F32
        )
    out_ref[0] = mine
    out_ref[1] = theirs


CHUNK = 9 * 128


def base_product(part, x, own, other):
    chunks = own.shape[1] // CHUNK
    begin, end = part * chunks // 2, (part + 1) * chunks // 2
    return pl.pallas_call(
        functools.partial(base_kernel, begin * CHUNK, (end - begin) * CHUNK),
        out_shape=jax.ShapeDtypeStruct((2, 64, 64), F32),
        in_specs=[VMEM] * 3,
        out_specs=VMEM,
        cost_estimate=pl.CostEstimate(flops=10**8, bytes_accessed=8 * 2**20, transcendentals=0),
        compiler_params=params(4),
        name=f"base_product_{part}",
    )(x, own, other)


def correct_kernel(base_0, base_1, x_ref, proj_ref, eh_ref, el_ref, fh_ref, fl_ref,
                   out_ref):
    p_high, p_low = split(proj_ref[...])
    e_high, e_low = eh_ref[...], el_ref[...]
    x = x_ref[:, : eh_ref.shape[0]]
    mine = base_0[0] + base_1[0]
    theirs = base_0[1] + base_1[1]
    first = lax.axis_index("tok") == 0
    base = jnp.concatenate(
        [jnp.where(first, mine, theirs), jnp.where(first, theirs, mine)], axis=1
    )
    base = base + (dot(x, fh_ref[...]) + dot(x, fl_ref[...]))
    fix = dot(p_high, e_high) + dot(p_high, e_low) + dot(p_low, e_high)
    out = (base - fix).astype(BF16)
    out_ref[...] = jnp.broadcast_to(out[None], out_ref.shape)


def correct(bases, x_all, projected, swept):
    return pl.pallas_call(
        correct_kernel,
        out_shape=jax.ShapeDtypeStruct((NZ, 64, 128), BF16),
        in_specs=[VMEM] * 8,
        out_specs=VMEM,
        cost_estimate=pl.CostEstimate(flops=10**7, bytes_accessed=2**20, transcendentals=0),
        compiler_params=params(4),
        name="correct",
    )(*bases, x_all, projected, *swept)


def lay_line_kernel(in_ref, low_ref, high_ref):
    for z in range(NZ):
        low_ref[:, z * 128 : (z + 1) * 128] = in_ref[z, :32, :]
        high_ref[:, z * 128 : (z + 1) * 128] = in_ref[z, 32:, :]


def lay_line(gathered):
    half = jax.ShapeDtypeStruct((32, NZ * 128), BF16)
    return pl.pallas_call(
        lay_line_kernel,
        out_shape=(half, half),
        in_specs=[VMEM],
        out_specs=(VMEM, VMEM),
        compiler_params=params(2),
        name="lay_line",
    )(gathered)


def place_kernel(mine, *refs):
    pieces, out_ref, sem = refs[:8], refs[-2], refs[-1]
    chip = lax.axis_index("rows")
    t = lax.axis_index("tok")
    y, x = chip // (NX * NZ), lax.rem(chip // NZ, NX)
    core = t if mine else 1 - t
    copies = []
    for part in range(2):
        x_first = part == 0
        rows = pl.ds(pl.multiple_of(core * 64 + part * 32, 32), 32)
        for second in range(4):
            for first in range(4):
                x_at = x ^ (first if x_first else second)
                y_at = y ^ (second if x_first else first)
                cols = pl.ds(pl.multiple_of((y_at * NX + x_at) * (NZ * 128), NZ * 128), NZ * 128)
                copies.append(
                    pltpu.make_async_copy(
                        pieces[part * 4 + second].at[first], out_ref.at[rows, cols],
                        sem.at[len(copies)],
                    )
                )
                copies[-1].start()
    for copy in copies:
        copy.wait()


def place(mine, pieces, out=None):
    extra = () if out is None else (out,)
    return pl.pallas_call(
        functools.partial(place_kernel, mine),
        out_shape=jax.ShapeDtypeStruct((128, CHIPS * 128), BF16),
        in_specs=[ANY] * (len(pieces) + len(extra)),
        out_specs=ANY,
        scratch_shapes=[pltpu.SemaphoreType.DMA((32,))],
        input_output_aliases={} if out is None else {len(pieces): 0},
        cost_estimate=pl.CostEstimate(flops=0, bytes_accessed=8 * 2**20, transcendentals=0),
        compiler_params=params(1),
        name="place_own" if mine else "place_other",
    )(*pieces, *extra)


def gather_output(copies):
    both = ("rows", "tok")
    line = [[chip_id(y, x, z) for z in range(NZ)] for y in range(NY) for x in range(NX)]
    halves = lay_line(lax.all_to_all(copies, "rows", 0, 0, axis_index_groups=line))

    def exchange(value, part, round_one):
        return [
            lax.ppermute(value, both, plane_pairs(o, (part == 0) == round_one)) for o in (1, 2, 3)
        ]

    blocks = [jnp.stack([h] + exchange(h, p, True)) for p, h in enumerate(halves)]
    mine = [piece for p, b in enumerate(blocks) for piece in [b] + exchange(b, p, False)]
    other = [lax.ppermute(piece, "tok", SWAP) for piece in mine]
    return place(False, other, place(True, mine))


def per_device(calib, w_panels, w_trail, keep_mask, factor_block, factor_trail):
    span = factor_block.shape[0]
    local = factor_trail.shape[1]
    chip = lax.axis_index("rows")

    panels_other = lax.ppermute(w_panels, "tok", SWAP)
    keep_other = lax.ppermute(keep_mask, "tok", SWAP)
    cols = lax.dynamic_slice_in_dim(calib, span + chip * local, local, 1)
    projected = lax.dot_general(cols, factor_trail, CONTRACT_LAST, preferred_element_type=F32)
    tie = lax.optimization_barrier
    projected, panels_other, keep_other, w_sent = tie(
        (projected, panels_other, keep_other, w_trail)
    )
    w_other = lax.ppermute(w_sent, "tok", SWAP)
    for step, (axis, bit) in enumerate(REDUCE_STEPS):
        received = lax.ppermute(projected, "rows", gray_pairs(axis, bit))
        if step == 0:
            prepared = prepare(w_panels, panels_other, keep_mask, keep_other, factor_block)
            *state, x_all = sweep_first(prepared, calib)
            projected, x_all, *state = tie((projected + received, x_all, *state))
        elif step == 1:
            state = sweep_middle(prepared, state)
            projected, *state = tie((projected + received, *state))
        elif step == 2:
            *swept, pruned, own_all = sweep_last(prepared, state, w_trail)
            projected, w_other, own_all, *swept = tie(
                (projected + received, w_other, own_all, *swept)
            )
        elif step == 3:
            bases = [base_product(part, x_all, own_all, w_other) for part in range(2)]
            projected, *bases = tie((projected + received, *bases))
        else:
            projected = projected + received
    return pruned, gather_output(correct(bases, x_all, projected, swept))


def solution(mesh):
    both = P(("rows", "tok"), None)
    return jax.shard_map(
        per_device,
        mesh=mesh,
        in_specs=(P("tok", None), both, both, both, P(), P(None, "rows")),
        out_specs=(both, P()),
        check_vma=False,
    )
```

```python
import functools

import jax
import jax.numpy as jnp
from jax import lax
from jax.experimental import pallas as pl
from jax.experimental.pallas import tpu as pltpu
from jax.sharding import PartitionSpec as P


NY, NX, NZ = 4, 4, 8
CHIPS = NY * NX * NZ
BLOCK = 16
PARTS = (5, 6)
F32 = jnp.float32
BF16 = jnp.bfloat16
VMEM = pl.BlockSpec(memory_space=pltpu.VMEM)
ANY = pl.BlockSpec(memory_space=pl.ANY)
HBM = pl.BlockSpec(memory_space=pltpu.MemorySpace.HBM)
CONTRACT_LAST = (((1,), (1,)), ((), ()))


def chip_id(y, x, z):
    return (y * NX + x) * NZ + z


def coords():
    return [(y, x, z) for y in range(NY) for x in range(NX) for z in range(NZ)]


def gray(i):
    return i ^ (i >> 1)


def gray_pairs(axis, bit):
    position = {gray(i): i for i in range(NZ)}
    pairs = []
    for here in coords():
        there = list(here)
        there[axis] = position[gray(here[axis]) ^ bit]
        pairs.append((chip_id(*here), chip_id(*there)))
    return pairs


REDUCE_STEPS = ((2, 1), (2, 2), (2, 4), (1, 1), (1, 2), (0, 1), (0, 2))


def plane_pairs(offset, first):
    pairs = []
    for y, x, z in coords():
        for t in range(2):
            peer = chip_id(y, x ^ offset, z) if first else chip_id(y ^ offset, x, z)
            pairs.append((chip_id(y, x, z) * 2 + t, peer * 2 + t))
    return pairs


SWAP = [(0, 1), (1, 0)]


def params(mib):
    return pltpu.CompilerParams(vmem_limit_bytes=mib * 2**20)


def split(v):
    high = v.astype(BF16)
    return high, (v - high.astype(F32)).astype(BF16)


def in_hbm(array):
    return pltpu.with_memory_space_constraint(array, pltpu.MemorySpace.HBM)


def dot(a, b):
    return jnp.dot(a, b, preferred_element_type=F32)


def prepare_kernel(w_own, w_other, keep_own, keep_other, factor_ref,
                   tiles, wt, scale, keep_t, fh, fl, w_all, keep_all, factor_all, sems):
    n = factor_ref.shape[0]
    own = pl.multiple_of(lax.axis_index("tok") * 64, 64)
    other = pl.multiple_of(64 - own, 64)
    loads = [
        pltpu.make_async_copy(factor_ref, factor_all, sems.at[0]),
        pltpu.make_async_copy(w_own, w_all.at[pl.ds(own, 64), :], sems.at[1]),
        pltpu.make_async_copy(keep_own, keep_all.at[pl.ds(own, 64), :], sems.at[2]),
    ]
    for load in loads:
        load.start()
    w_all[pl.ds(other, 64), :] = w_other[...]
    keep_all[pl.ds(other, 64), :] = keep_other[...]
    for load in loads:
        load.wait()
    factor = factor_all[...]
    for block in range(n // BLOCK):
        rows, lanes = block * BLOCK, block * BLOCK // 128 * 128
        tiles[block] = factor_all[rows : rows + BLOCK, lanes : lanes + 128]
    eye = (lax.broadcasted_iota(jnp.int32, (n, n), 0) == lax.broadcasted_iota(jnp.int32, (n, n), 1))
    diag = jnp.sum(jnp.where(eye, factor, 0.0), axis=1, keepdims=True)
    ft_high, ft_low = split(factor.T)
    fh[...] = ft_high
    fl[...] = ft_low
    wt[...] = w_all[...].astype(F32).T
    kept = keep_all[...].astype(F32).T
    keep_t[...] = kept
    scale[...] = (1.0 - kept) * (1.0 / diag)


def prepare(w_own, w_other, keep_own, keep_other, factor):
    n = factor.shape[0]
    tall = jax.ShapeDtypeStruct((n, 128), F32)
    square = jax.ShapeDtypeStruct((n, n), BF16)
    tiles = jax.ShapeDtypeStruct((n // BLOCK, BLOCK, 128), F32)
    return pl.pallas_call(
        prepare_kernel,
        out_shape=(tiles, tall, tall, tall, square, square),
        in_specs=[HBM, VMEM, HBM, VMEM, HBM],
        out_specs=(VMEM,) * 6,
        scratch_shapes=[
            pltpu.VMEM((128, n), BF16),
            pltpu.VMEM((128, n), jnp.int32),
            pltpu.VMEM((n, n), F32),
            pltpu.SemaphoreType.DMA((3,)),
        ],
        cost_estimate=pl.CostEstimate(flops=10**8, bytes_accessed=6 * 2**20, transcendentals=0),
        compiler_params=params(4),
        name="prepare",
    )(in_hbm(w_own), w_other, in_hbm(keep_own), keep_other, in_hbm(factor))


def sweep_blocks(first, count, tiles_ref, wt, scale, keep_t, fh, fl, eh, el, final_t, cur, tiles,
                 tile_sem):
    sub = lax.broadcasted_iota(jnp.int32, (BLOCK, 128), 0)

    def tile_copy(block):
        return pltpu.make_async_copy(
            tiles_ref.at[block], tiles.at[block - first], tile_sem.at[block - first]
        )

    for block in range(first, first + count):
        tile_copy(block).start()

    def advance(block, carry):
        start = pl.multiple_of(block * BLOCK, BLOCK)
        lane = lax.rem(start, 128)
        rows = pl.ds(start, BLOCK)
        tile_copy(block).wait()
        high, low = fh[rows, :], fl[rows, :]
        errs_high = eh[...]
        update = dot(high, errs_high) + dot(low, errs_high) + dot(high, el[...])
        cur[...] = wt[rows, :] - update
        cols = [cur[pl.ds(j, 8, stride=0), :] for j in range(BLOCK)]
        errs = jnp.zeros((BLOCK, 128), F32)
        vals = jnp.zeros((BLOCK, 128), F32)
        for j in range(BLOCK):
            e = cols[j] * scale[pl.ds(start + j, 8, stride=0), :]
            for k in range(j + 1, BLOCK):
                cols[k] = cols[k] - e * tiles[block - first, j, lane + k]
            wide_e = jnp.concatenate([e] * (BLOCK // 8), axis=0)
            wide_c = jnp.concatenate([cols[j]] * (BLOCK // 8), axis=0)
            errs = jnp.where(sub == j, wide_e, errs)
            vals = jnp.where(sub == j, wide_c, vals)
        final_t[rows, :] = vals * keep_t[rows, :]
        e_high, e_low = split(errs)
        eh[rows, :] = e_high
        el[rows, :] = e_low
        return carry

    lax.fori_loop(first, first + count, advance, 0)


def sweep_first_kernel(tiles_ref, wt, scale, keep_t, fh, fl, calib_ref, eh, el, final_t, x_out,
                       cur, tiles, sem, load_sem):
    load = pltpu.make_async_copy(calib_ref, x_out, load_sem)
    load.start()
    eh[...] = jnp.zeros_like(eh)
    el[...] = jnp.zeros_like(el)
    final_t[...] = jnp.zeros_like(final_t)
    sweep_blocks(0, PARTS[0], tiles_ref, wt, scale, keep_t, fh, fl, eh, el, final_t, cur, tiles, sem)
    load.wait()


def sweep_middle_kernel(tiles_ref, wt, scale, keep_t, fh, fl, eh_in, el_in, final_in,
                        eh, el, final_t, cur, tiles, sem):
    eh[...] = eh_in[...]
    el[...] = el_in[...]
    final_t[...] = final_in[...]
    sweep_blocks(PARTS[0], PARTS[1], tiles_ref, wt, scale, keep_t, fh, fl, eh, el, final_t, cur,
                 tiles, sem)


def sweep_last_kernel(tiles_ref, wt, scale, keep_t, fh, fl, eh_in, el_in, final_in, trail_ref,
                      eh, el, fin_high, fin_low, pruned_ref, trail_out,
                      final_t, back, cur, tiles, sem, load_sem):
    load = pltpu.make_async_copy(trail_ref, trail_out, load_sem)
    load.start()
    own = pl.multiple_of(lax.axis_index("tok") * 64, 64)
    eh[...] = eh_in[...]
    el[...] = el_in[...]
    final_t[...] = final_in[...]
    done = PARTS[0] + PARTS[1]
    sweep_blocks(done, tiles_ref.shape[0] - done, tiles_ref, wt, scale, keep_t, fh, fl, eh, el,
                 final_t, cur, tiles, sem)
    final = final_t[...]
    high, low = split(final)
    fin_high[...] = high
    fin_low[...] = low
    back[...] = final.T
    pruned_ref[...] = back[pl.ds(own, 64), :].astype(BF16)
    load.wait()


def sweep_scratch(count):
    return [
        pltpu.VMEM((BLOCK, 128), F32),
        pltpu.SMEM((count, BLOCK, 128), F32),
        pltpu.SemaphoreType.DMA((count,)),
    ]


SWEEP_COST = pl.CostEstimate(flops=10**8, bytes_accessed=8 * 2**20, transcendentals=0)


def sweep_first(prepared, calib):
    n = prepared[0].shape[0] * BLOCK
    narrow = jax.ShapeDtypeStruct((n, 128), BF16)
    return pl.pallas_call(
        sweep_first_kernel,
        out_shape=(
            narrow, narrow, jax.ShapeDtypeStruct((n, 128), F32),
            jax.ShapeDtypeStruct(calib.shape, BF16),
        ),
        in_specs=[VMEM] * 6 + [HBM],
        out_specs=(VMEM,) * 4,
        scratch_shapes=sweep_scratch(PARTS[0]) + [pltpu.SemaphoreType.DMA],
        cost_estimate=SWEEP_COST,
        compiler_params=params(10),
        name="sweep_first",
    )(*prepared, in_hbm(calib))


def sweep_middle(prepared, state):
    n = prepared[0].shape[0] * BLOCK
    narrow = jax.ShapeDtypeStruct((n, 128), BF16)
    return pl.pallas_call(
        sweep_middle_kernel,
        out_shape=(narrow, narrow, jax.ShapeDtypeStruct((n, 128), F32)),
        in_specs=[VMEM] * 9,
        out_specs=(VMEM,) * 3,
        scratch_shapes=sweep_scratch(PARTS[1]),
        cost_estimate=SWEEP_COST,
        compiler_params=params(6),
        name="sweep_middle",
    )(*prepared, *state)


def sweep_last(prepared, state, w_trail):
    n = prepared[0].shape[0] * BLOCK
    narrow = jax.ShapeDtypeStruct((n, 128), BF16)
    count = prepared[0].shape[0] - PARTS[0] - PARTS[1]
    return pl.pallas_call(
        sweep_last_kernel,
        out_shape=(narrow,) * 4
        + (jax.ShapeDtypeStruct((64, n), BF16), jax.ShapeDtypeStruct(w_trail.shape, BF16)),
        in_specs=[VMEM] * 9 + [HBM],
        out_specs=(VMEM,) * 6,
        scratch_shapes=[pltpu.VMEM((n, 128), F32), pltpu.VMEM((128, n), F32)]
        + sweep_scratch(count)
        + [pltpu.SemaphoreType.DMA],
        cost_estimate=SWEEP_COST,
        compiler_params=params(10),
        name="sweep_last",
    )(*prepared, *state, in_hbm(w_trail))


def base_kernel(begin, width, x_ref, own_ref, other_ref, out_ref):
    skip = x_ref.shape[1] - own_ref.shape[1]
    mine = jnp.zeros((64, 64), F32)
    theirs = jnp.zeros((64, 64), F32)
    for at in range(begin, begin + width, CHUNK):
        x = x_ref[:, skip + at : skip + at + CHUNK]
        cols = slice(at, at + CHUNK)
        mine = mine + lax.dot_general(
            x, own_ref[:, cols], CONTRACT_LAST, preferred_element_type=F32
        )
        theirs = theirs + lax.dot_general(
            x, other_ref[:, cols], CONTRACT_LAST, preferred_element_type=F32
        )
    out_ref[0] = mine
    out_ref[1] = theirs


CHUNK = 9 * 128


def base_product(part, x, own, other):
    chunks = own.shape[1] // CHUNK
    begin, end = part * chunks // 2, (part + 1) * chunks // 2
    return pl.pallas_call(
        functools.partial(base_kernel, begin * CHUNK, (end - begin) * CHUNK),
        out_shape=jax.ShapeDtypeStruct((2, 64, 64), F32),
        in_specs=[VMEM] * 3,
        out_specs=VMEM,
        cost_estimate=pl.CostEstimate(flops=10**8, bytes_accessed=8 * 2**20, transcendentals=0),
        compiler_params=params(4),
        name=f"base_product_{part}",
    )(x, own, other)


def correct_kernel(base_0, base_1, x_ref, proj_ref, eh_ref, el_ref, fh_ref, fl_ref,
                   out_ref):
    p_high, p_low = split(proj_ref[...])
    e_high, e_low = eh_ref[...], el_ref[...]
    x = x_ref[:, : eh_ref.shape[0]]
    mine = base_0[0] + base_1[0]
    theirs = base_0[1] + base_1[1]
    first = lax.axis_index("tok") == 0
    base = jnp.concatenate(
        [jnp.where(first, mine, theirs), jnp.where(first, theirs, mine)], axis=1
    )
    base = base + (dot(x, fh_ref[...]) + dot(x, fl_ref[...]))
    fix = dot(p_high, e_high) + dot(p_high, e_low) + dot(p_low, e_high)
    out = (base - fix).astype(BF16)
    out_ref[...] = jnp.broadcast_to(out[None], out_ref.shape)


def correct(bases, x_all, projected, swept):
    return pl.pallas_call(
        correct_kernel,
        out_shape=jax.ShapeDtypeStruct((NZ, 64, 128), BF16),
        in_specs=[VMEM] * 8,
        out_specs=VMEM,
        cost_estimate=pl.CostEstimate(flops=10**7, bytes_accessed=2**20, transcendentals=0),
        compiler_params=params(4),
        name="correct",
    )(*bases, x_all, projected, *swept)


def lay_line_kernel(in_ref, low_ref, high_ref):
    for z in range(NZ):
        low_ref[:, z * 128 : (z + 1) * 128] = in_ref[z, :32, :]
        high_ref[:, z * 128 : (z + 1) * 128] = in_ref[z, 32:, :]


def lay_line(gathered):
    half = jax.ShapeDtypeStruct((32, NZ * 128), BF16)
    return pl.pallas_call(
        lay_line_kernel,
        out_shape=(half, half),
        in_specs=[VMEM],
        out_specs=(VMEM, VMEM),
        compiler_params=params(2),
        name="lay_line",
    )(gathered)


def place_kernel(mine, *refs):
    pieces, out_ref, sem = refs[:8], refs[-2], refs[-1]
    chip = lax.axis_index("rows")
    t = lax.axis_index("tok")
    y, x = chip // (NX * NZ), lax.rem(chip // NZ, NX)
    core = t if mine else 1 - t
    copies = []
    for part in range(2):
        x_first = part == 0
        rows = pl.ds(pl.multiple_of(core * 64 + part * 32, 32), 32)
        for second in range(4):
            for first in range(4):
                x_at = x ^ (first if x_first else second)
                y_at = y ^ (second if x_first else first)
                cols = pl.ds(pl.multiple_of((y_at * NX + x_at) * (NZ * 128), NZ * 128), NZ * 128)
                copies.append(
                    pltpu.make_async_copy(
                        pieces[part * 4 + second].at[first], out_ref.at[rows, cols],
                        sem.at[len(copies)],
                    )
                )
                copies[-1].start()
    for copy in copies:
        copy.wait()


def place(mine, pieces, out=None):
    extra = () if out is None else (out,)
    return pl.pallas_call(
        functools.partial(place_kernel, mine),
        out_shape=jax.ShapeDtypeStruct((128, CHIPS * 128), BF16),
        in_specs=[ANY] * (len(pieces) + len(extra)),
        out_specs=ANY,
        scratch_shapes=[pltpu.SemaphoreType.DMA((32,))],
        input_output_aliases={} if out is None else {len(pieces): 0},
        cost_estimate=pl.CostEstimate(flops=0, bytes_accessed=8 * 2**20, transcendentals=0),
        compiler_params=params(1),
        name="place_own" if mine else "place_other",
    )(*pieces, *extra)


def gather_output(copies):
    both = ("rows", "tok")
    line = [[chip_id(y, x, z) for z in range(NZ)] for y in range(NY) for x in range(NX)]
    halves = lay_line(lax.all_to_all(copies, "rows", 0, 0, axis_index_groups=line))

    def exchange(value, part, round_one):
        return [
            lax.ppermute(value, both, plane_pairs(o, (part == 0) == round_one)) for o in (1, 2, 3)
        ]

    blocks = [jnp.stack([h] + exchange(h, p, True)) for p, h in enumerate(halves)]
    mine = [piece for p, b in enumerate(blocks) for piece in [b] + exchange(b, p, False)]
    other = [lax.ppermute(piece, "tok", SWAP) for piece in mine]
    return place(False, other, place(True, mine))


def per_device(calib, w_panels, w_trail, keep_mask, factor_block, factor_trail):
    span = factor_block.shape[0]
    local = factor_trail.shape[1]
    chip = lax.axis_index("rows")

    panels_other = lax.ppermute(w_panels, "tok", SWAP)
    keep_other = lax.ppermute(keep_mask, "tok", SWAP)
    cols = lax.dynamic_slice_in_dim(calib, span + chip * local, local, 1)
    projected = lax.dot_general(cols, factor_trail, CONTRACT_LAST, preferred_element_type=F32)
    tie = lax.optimization_barrier
    projected, panels_other, keep_other, w_sent = tie(
        (projected, panels_other, keep_other, w_trail)
    )
    w_other = lax.ppermute(w_sent, "tok", SWAP)
    for step, (axis, bit) in enumerate(REDUCE_STEPS):
        received = lax.ppermute(projected, "rows", gray_pairs(axis, bit))
        if step == 0:
            prepared = prepare(w_panels, panels_other, keep_mask, keep_other, factor_block)
            projected, *prepared = tie((projected + received, *prepared))
        elif step == 1:
            *state, x_all = sweep_first(prepared, calib)
            projected, x_all, *state = tie((projected + received, x_all, *state))
        elif step == 2:
            state = sweep_middle(prepared, state)
            projected, *state = tie((projected + received, *state))
        elif step == 3:
            *swept, pruned, own_all = sweep_last(prepared, state, w_trail)
            projected, w_other, own_all, *swept = tie(
                (projected + received, w_other, own_all, *swept)
            )
        elif step == 4:
            bases = [base_product(part, x_all, own_all, w_other) for part in range(2)]
            projected, *bases = tie((projected + received, *bases))
        else:
            projected = projected + received
    return pruned, gather_output(correct(bases, x_all, projected, swept))


def solution(mesh):
    both = P(("rows", "tok"), None)
    return jax.shard_map(
        per_device,
        mesh=mesh,
        in_specs=(P("tok", None), both, both, both, P(), P(None, "rows")),
        out_specs=(both, P()),
        check_vma=False,
    )
```
